256 devices in a mesh: wide: 64 (over y, z, core), narrow: 4 (over x).
Axes of the slice: x: 4, y: 4, z: 8, core: 2. Of those that a mesh axis runs over, the one named last changes fastest.
Arguments:
- diag_block: float32 [256, 512, 512], P('wide', None, 'narrow'), as said below
- panel: float32 [256, 1024, 512], P('wide', None, 'narrow'), may hold values from -2 to 2
- panel_count: int32 [256], P('wide'), may hold values from 1 to 8, 1152 in all
- pair_owner: int32 [9216, 1], P('wide'), may hold values from 0 to 63; in each aligned block of 144 rows (0 to 143, 144 to 287, ...) at most 3 rows name the same one
- pair_slot: int32 [9216], P('wide'), may hold values from 0 to 7
- ancestor: float32 [512, 128, 128], P(('wide', 'narrow')), may hold values from -6 to 6
Outputs:
- factor: float32 [256, 512, 512], P('wide', None, 'narrow')
- lower_panel: float32 [256, 1024, 512], P('wide', None, 'narrow')
- updated: float32 [512, 128, 128], P(('wide', 'narrow'))
The draws below stay inside these ranges and needn't reach their ends.
Inputs may be any that keep to these rules, and one draw needn't show every extreme that they name: Each diag_block[s] is symmetric, and its least eigenvalue is 0.2 or more. `pair_owner`: among the rows of one index of wide no owner is named more than 3 times, a bound that some block reaches.
All inputs are finite; a program needn't handle non-finite values. No bound on the sum of `panel_count` on one device may be relied on, other than what follows from the above.
Results may differ from the reference program's by a relative error of at most 0.00016.
Values sent between devices are 32-bit elements; how exact they have to be, the bound alone decides.
A program may use at most 128 MiB of HBM per device.

```python
import math
import jax
import jax.numpy as jnp
import numpy as np
from jax import lax

W = 512
B = 128
P_SIZE = 8
T_DEV = 2
SUPERS = 256
TILES = 512
NPAIR = 36
ROWS_DEV = 144
CAP = 3
N_WIDE = 64
N_NARROW = 4


def draw_diag_block(key, part):
    first_key = jax.random.fold_in(jax.random.fold_in(key, 7), 0)
    factors = jax.random.normal(first_key, (SUPERS, W, W), jnp.float32)
    scales = jnp.ones((SUPERS, W, 1), jnp.float32)
    gram = jnp.einsum('sik,sjk->sij', factors, factors, precision=lax.Precision.HIGHEST) * (1.0 / W)
    gram = 0.5 * (gram + jnp.swapaxes(gram, 1, 2))
    identity = jnp.eye(W, dtype=jnp.float32)
    shifted = gram + 0.2 * identity
    return shifted * jnp.swapaxes(scales, 1, 2)


def set_ends(drawn, own_key, smallest, largest):
    longest = drawn.shape.index(max(drawn.shape))
    spots = []
    for shift in (0, 1):
        where = [jax.random.randint(jax.random.fold_in(own_key, axis), (), 0, length) for axis, length in enumerate(drawn.shape)]
        where[longest] = (where[longest] + shift) % drawn.shape[longest]
        spots.append(tuple(where))
    return drawn.at[spots[0]].set(smallest).at[spots[1]].set(largest)


def steps_of(own_key, dims, shards, least, largest):
    def one(position, blocks):
        draws = jax.random.uniform(jax.random.fold_in(jax.random.fold_in(own_key, 6), position), (blocks,), jnp.float32, least / len(shards), largest / len(shards))
        return jnp.repeat(jnp.exp(draws), dims[position] // blocks).reshape((-1,) + (1,) * (len(dims) - position - 1))

    factor_of = one(*shards[0])
    for cut in shards[1:]:
        factor_of = factor_of * one(*cut)
    return factor_of


def length_profile(amount, total, bound, slope):
    portions = [(1 << 20) // math.isqrt(standing ** slope) + 1 for standing in range(2, amount + 1)]
    surplus, holding = total - bound - (amount - 1), [1] * (amount - 1)
    while surplus > 0:
        free = [i for i in range(amount - 1) if holding[i] < bound]
        whole, left = sum([portions[i] for i in free]), surplus
        for i in free:
            extra = min(bound - holding[i], max(1, left * portions[i] // whole), surplus)
            holding[i] = holding[i] + extra
            surplus = surplus - extra
    return np.array([bound] + holding)


def ragged(key, number_of, total, most, lean):
    if number_of == 2:
        one = jax.random.randint(key, (), max(1, total - most), min(most, total - 1) + 1)
        return jnp.stack([one, total - one])
    lengths = jnp.asarray(length_profile(number_of, total, most, lean), jnp.int32)
    couples = (number_of - 1) // 2
    giver, sink = lengths[1:1 + 2 * couples:2], lengths[2:2 + 2 * couples:2]
    margin = jnp.minimum(giver - 1, most - sink)
    passed = jax.random.randint(jax.random.fold_in(key, 1), (couples,), 0, 1 << 20) % (margin + 1)
    lengths = lengths.at[1:1 + 2 * couples:2].set(giver - passed).at[2:2 + 2 * couples:2].set(sink + passed)
    return lengths[jax.random.permutation(jax.random.fold_in(key, 2), number_of)]


def assign_block(rng, own, number, rows, count, top, limit, slope):
    sequence = jax.random.permutation(rng, count)
    packed, ordinary = portions_of(count, rows * top, limit, slope, True), portions_of(count, rows * top, limit, slope, False)
    places = jnp.arange(count)

    def named(sizes, rotation):
        used = int((sizes > 0).sum())
        fixed = max(1, used // 4)
        moved = fixed + (places - fixed + rotation * (used - fixed)) % max(1, count - fixed)
        return jnp.zeros((count,), jnp.int32).at[sequence[jnp.where(places < fixed, places, moved)]].set(jnp.asarray(sizes, jnp.int32))

    sizes = jnp.where(number % 4 == 0, named(packed, number // 4), named(ordinary, number - number // 4 - 1))
    mixed = jax.random.permutation(jax.random.fold_in(own, 3), count)
    giver, sink = mixed[0:count // 2 * 2:2], mixed[1:count // 2 * 2:2]
    margin = jnp.minimum(sizes[giver] - 1, limit - sizes[sink]) // 2
    margin = jnp.where((giver == sequence[0]) | (sink == sequence[0]) | (sizes[sink] == 0), 0, jnp.maximum(margin, 0))
    moved = jax.random.randint(jax.random.fold_in(own, 4), (count // 2,), 0, 1 << 20) % (margin + 1)
    sizes = sizes.at[giver].add(-moved).at[sink].add(moved)
    items = jnp.searchsorted(jnp.cumsum(sizes), jnp.arange(rows * top), side="right").astype(jnp.int32)
    table = items.reshape(top, rows).T
    table = table[jax.random.permutation(jax.random.fold_in(own, 1), rows)]
    rotation = jax.random.randint(jax.random.fold_in(own, 2), (rows, 1), 0, top)
    return jnp.take_along_axis(table, (jnp.arange(top)[None, :] + rotation) % top, axis=1)


def portions_of(number_of, total, bound, slope, full):
    portions = [(1 << 20) // math.isqrt(rank ** slope) + 1 for rank in range(1, number_of + 1)]
    largest = bound if full else min(bound, max(-(-total // number_of), total * portions[0] // sum(portions)))
    least = 1 if total - largest >= number_of - 1 else 0
    holding, rest = [largest] + [least] * (number_of - 1), total - largest - least * (number_of - 1)
    while rest > 0:
        movable = [i for i in range(1, number_of) if holding[i] < largest] or [i for i in range(1, number_of) if holding[i] < bound]
        pool, remaining = sum([portions[i] for i in movable]), rest
        for i in movable:
            addition = min(bound - holding[i], max(1, remaining * portions[i] // pool), rest)
            holding[i] = holding[i] + addition
            rest = rest - addition
    return np.array(holding)


def noise(own_key, shape, spread, reach, cuts=(), kind=jnp.bfloat16):
    drawn = spread * jax.random.normal(own_key, shape, jnp.float32)
    if cuts:
        drawn = drawn * steps_of(own_key, shape, cuts, -0.22, 0.18)
    return jnp.clip(drawn, -reach, reach).astype(kind)


def setup_inputs(seed: int = 0) -> dict:
    key_of = jax.random.split(jax.random.key(seed), 7)
    diag_block = draw_diag_block(jax.random.fold_in(key_of[6], 71), 0)
    panel = noise(key_of[1], (SUPERS, P_SIZE * B, W), 0.15, 2.0, ((0, 64), (2, 4)), jnp.float32)
    panel_count = ragged(key_of[2], SUPERS, SUPERS * (P_SIZE + 1) // 2, P_SIZE, 2).astype(jnp.int32)
    pair_owner_keys = jax.random.split(jax.random.fold_in(key_of[3], 1), (SUPERS * NPAIR) // ROWS_DEV)
    pair_owner_turns = jax.random.permutation(jax.random.fold_in(key_of[3], 3), (SUPERS * NPAIR) // ROWS_DEV)
    pair_owner = jax.vmap(lambda own, number: assign_block(jax.random.fold_in(key_of[3], 2), own, number, ROWS_DEV, N_WIDE, 1, CAP, 2))(pair_owner_keys, pair_owner_turns).reshape((SUPERS * NPAIR, 1))
    pair_slot = set_ends(jax.random.randint(key_of[4], (SUPERS * NPAIR,), 0, T_DEV * N_NARROW), jax.random.fold_in(key_of[4], 1), 0, (T_DEV * N_NARROW) - 1).astype(jnp.int32)
    ancestor = noise(key_of[5], (TILES, B, B), 1.0, 6.0, ((0, 256),), jnp.float32)
    return dict(diag_block=diag_block, panel=panel, panel_count=panel_count, pair_owner=pair_owner, pair_slot=pair_slot, ancestor=ancestor)


def pair_lists(count):
    first = []
    second = []
    for outer in range(count):
        for inner in range(outer + 1):
            first.append(outer)
            second.append(inner)
    return (np.array(first, np.int32), np.array(second, np.int32))

def reference(diag_block, panel, panel_count, pair_owner, pair_slot, ancestor):
    factor = jnp.linalg.cholesky(diag_block)
    identity = jnp.broadcast_to(jnp.eye(W, dtype=jnp.float32), factor.shape)
    inverse = lax.linalg.triangular_solve(factor, identity, left_side=True, lower=True)
    lower_panel = jnp.einsum('srk,sck->src', panel, inverse, precision=lax.Precision.HIGHEST)
    block_index = jnp.arange(P_SIZE * B, dtype=jnp.int32) // B
    live = (block_index[None, :] < panel_count[:, None]).astype(jnp.float32)
    lower_panel = lower_panel * live[:, :, None]
    first, second = pair_lists(P_SIZE)
    target = pair_owner[:, 0] * (T_DEV * N_NARROW) + pair_slot
    target = target.reshape(SUPERS, NPAIR).astype(jnp.int32)

    def one_super(tiles, items):
        rows, goal = items
        blocks = rows.reshape(P_SIZE, B, W)
        contribution = jnp.einsum('pac,pbc->pab', blocks[first], blocks[second], precision=lax.Precision.HIGHEST)
        return (tiles.at[goal].add(contribution), None)
    summed, _ = lax.scan(one_super, jnp.zeros(ancestor.shape, jnp.float32), (lower_panel, target))
    return (factor, lower_panel, ancestor - summed)
```

```python
import jax
import jax.numpy as jnp
import numpy as np
from jax import lax
from jax.sharding import PartitionSpec as P

W = 512
B = 128
P_SIZE = 8
T_DEV = 2


def pair_lists(count):
    first = []
    second = []
    for outer in range(count):
        for inner in range(outer + 1):
            first.append(outer)
            second.append(inner)
    return (np.array(first, np.int32), np.array(second, np.int32))


def local(diag_block, panel, panel_count, pair_owner, pair_slot, ancestor):
    supers_here = diag_block.shape[0]
    col_width = diag_block.shape[2]
    diag_rows = diag_block.shape[1]
    narrow_index = lax.axis_index("narrow")
    narrow_count = lax.axis_size("narrow")
    wide_count = lax.axis_size("wide")
    group = supers_here // narrow_count

    stacked = jnp.concatenate([diag_block, panel], axis=1)
    whole = lax.all_to_all(stacked, "narrow", split_axis=0, concat_axis=2, tiled=True)
    whole_diag = whole[:, :diag_rows, :]
    whole_panel = whole[:, diag_rows:, :]

    factor = jnp.linalg.cholesky(whole_diag)
    identity = jnp.broadcast_to(jnp.eye(W, dtype=jnp.float32), factor.shape)
    inverse = lax.linalg.triangular_solve(factor, identity, left_side=True, lower=True)
    lower_panel = jnp.einsum(
        "srk,sck->src", whole_panel, inverse, precision=lax.Precision.HIGHEST
    )
    counts = lax.dynamic_slice_in_dim(panel_count, narrow_index * group, group)
    block_index = jnp.arange(P_SIZE * B, dtype=jnp.int32) // B
    live = (block_index[None, :] < counts[:, None]).astype(jnp.float32)
    lower_panel = lower_panel * live[:, :, None]

    first, second = pair_lists(P_SIZE)
    npair = len(first)
    blocks = lower_panel.reshape(group, P_SIZE, B, W)
    contribution = jnp.einsum(
        "spac,spbc->spab", blocks[:, first], blocks[:, second], precision=lax.Precision.HIGHEST
    )

    done = jnp.concatenate([factor, lower_panel], axis=1)
    back = lax.all_to_all(done, "narrow", split_axis=2, concat_axis=0, tiled=True)
    factor_cols = back[:, :diag_rows, :]
    lower_cols = back[:, diag_rows:, :]

    quarters = lax.all_to_all(contribution, "narrow", split_axis=2, concat_axis=0, tiled=True)
    quarter_rows = quarters.shape[2]
    pair_rows = supers_here * npair
    quarters = quarters.reshape(pair_rows, quarter_rows, B)

    capacity = max(2, (pair_rows + wide_count - 1) // wide_count)
    owners = pair_owner[:, 0]
    owner_table = (owners[:, None] == jnp.arange(wide_count, dtype=jnp.int32)[None, :]).astype(
        jnp.int32
    )
    earlier = jnp.cumsum(owner_table, axis=0) - owner_table
    rank_here = jnp.sum(earlier * owner_table, axis=1)
    position = owners * capacity + rank_here
    buffer_rows = wide_count * capacity
    row_slots = T_DEV * narrow_count
    slot_ids = jnp.full((buffer_rows,), -1, jnp.int32).at[position].set(pair_slot)
    source_row = jnp.zeros((buffer_rows,), jnp.int32).at[position].set(
        jnp.arange(pair_rows, dtype=jnp.int32)
    )
    filled = jnp.zeros((buffer_rows,), jnp.bool_).at[position].set(True)
    send_buffer = jnp.where(filled[:, None, None], quarters[source_row], 0.0)
    received = lax.all_to_all(send_buffer, "wide", split_axis=0, concat_axis=0, tiled=True)
    got_slots = lax.all_to_all(slot_ids, "wide", split_axis=0, concat_axis=0, tiled=True)
    slot_table = (got_slots[:, None] == jnp.arange(row_slots, dtype=jnp.int32)[None, :]).astype(
        jnp.float32
    )
    slot_sums = jnp.einsum("ri,rab->iab", slot_table, received, precision=lax.Precision.HIGHEST)
    slot_sums = slot_sums.reshape(narrow_count, T_DEV, quarter_rows, B)
    summed = lax.all_to_all(slot_sums, "narrow", split_axis=0, concat_axis=2, tiled=True)
    summed = summed.reshape(T_DEV, B, B)
    return (factor_cols, lower_cols, ancestor - summed)


def solution(mesh):
    placed = (
        P("wide", None, "narrow"),
        P("wide", None, "narrow"),
        P("wide"),
        P("wide", None),
        P("wide"),
        P(("wide", "narrow"), None, None),
    )
    return jax.shard_map(
        local,
        mesh=mesh,
        in_specs=placed,
        out_specs=(
            P("wide", None, "narrow"),
            P("wide", None, "narrow"),
            P(("wide", "narrow"), None, None),
        ),
        check_vma=False,
    )
```

```python
import jax
import jax.numpy as jnp
import numpy as np
from jax import lax
from jax.sharding import PartitionSpec as P

W = 512
B = 128
P_SIZE = 8
T_DEV = 2


def pair_lists(count):
    first = []
    second = []
    for outer in range(count):
        for inner in range(outer + 1):
            first.append(outer)
            second.append(inner)
    return (np.array(first, np.int32), np.array(second, np.int32))


def mm(a, b):
    return jnp.einsum("sik,skj->sij", a, b, precision=lax.Precision.HIGHEST)


def mm_t(a, b):
    return jnp.einsum("sik,sjk->sij", a, b, precision=lax.Precision.HIGHEST)


def blocked_cholesky(matrix):
    batch, size, _ = matrix.shape
    nblk = size // B
    eye = jnp.broadcast_to(jnp.eye(B, dtype=jnp.float32), (batch, B, B))
    trailing = matrix
    diag_l, diag_inv, below = [], [], []
    inverse_rows = []
    for k in range(nblk):
        head = trailing[:, :B, :B]
        l_kk = lax.linalg.cholesky(head, symmetrize_input=False)
        i_kk = lax.linalg.triangular_solve(l_kk, eye, left_side=True, lower=True)
        diag_l.append(l_kk)
        diag_inv.append(i_kk)
        if k > 0:
            left = jnp.concatenate([below[j][:, (k - j - 1) * B:(k - j) * B, :] for j in range(k)], axis=2)
            upper = jnp.concatenate(inverse_rows, axis=1)
            rest = -mm(left, upper)
            rest = jnp.concatenate([rest[:, :, :k * B], eye, rest[:, :, (k + 1) * B:]], axis=2)
            inverse_rows.append(mm(i_kk, rest))
        else:
            inverse_rows.append(jnp.concatenate(
                [i_kk, jnp.zeros((batch, B, size - B), jnp.float32)], axis=2))
        if k < nblk - 1:
            panel_k = mm_t(trailing[:, B:, :B], i_kk)
            below.append(panel_k)
            trailing = trailing[:, B:, B:] - mm_t(panel_k, panel_k)
    columns = []
    for k in range(nblk):
        parts = []
        if k > 0:
            parts.append(jnp.zeros((batch, k * B, B), jnp.float32))
        parts.append(diag_l[k])
        if k < nblk - 1:
            parts.append(below[k])
        columns.append(jnp.concatenate(parts, axis=1))
    factor = jnp.concatenate(columns, axis=2)
    inverse = jnp.concatenate(inverse_rows, axis=1)
    return factor, inverse


def local(diag_block, panel, panel_count, pair_owner, pair_slot, ancestor):
    supers_here = diag_block.shape[0]
    col_width = diag_block.shape[2]
    diag_rows = diag_block.shape[1]
    narrow_index = lax.axis_index("narrow")
    narrow_count = lax.axis_size("narrow")
    wide_count = lax.axis_size("wide")
    group = supers_here // narrow_count

    whole_diag = lax.all_to_all(diag_block, "narrow", split_axis=0, concat_axis=2, tiled=True)
    whole_panel = lax.all_to_all(panel, "narrow", split_axis=0, concat_axis=2, tiled=True)

    factor, inverse = blocked_cholesky(whole_diag)
    factor_back = lax.all_to_all(factor, "narrow", split_axis=2, concat_axis=0, tiled=True)
    lower_panel = jnp.einsum(
        "srk,sck->src", whole_panel, inverse, precision=lax.Precision.HIGHEST
    )
    counts = lax.dynamic_slice_in_dim(panel_count, narrow_index * group, group)
    block_index = jnp.arange(P_SIZE * B, dtype=jnp.int32) // B
    live = (block_index[None, :] < counts[:, None]).astype(jnp.float32)
    lower_panel = lower_panel * live[:, :, None]
    lower_back = lax.all_to_all(lower_panel, "narrow", split_axis=2, concat_axis=0, tiled=True)

    first, second = pair_lists(P_SIZE)
    npair = len(first)
    blocks = lower_panel.reshape(group, P_SIZE, B, W)
    contribution = jnp.einsum(
        "spac,spbc->spab", blocks[:, first], blocks[:, second], precision=lax.Precision.HIGHEST
    )

    quarters = lax.all_to_all(contribution, "narrow", split_axis=2, concat_axis=0, tiled=True)
    quarter_rows = quarters.shape[2]
    pair_rows = supers_here * npair
    quarters = quarters.reshape(pair_rows, quarter_rows, B)

    capacity = max(2, (pair_rows + wide_count - 1) // wide_count)
    owners = pair_owner[:, 0]
    owner_table = (owners[:, None] == jnp.arange(wide_count, dtype=jnp.int32)[None, :]).astype(
        jnp.int32
    )
    earlier = jnp.cumsum(owner_table, axis=0) - owner_table
    rank_here = jnp.sum(earlier * owner_table, axis=1)
    position = owners * capacity + rank_here
    buffer_rows = wide_count * capacity
    row_slots = T_DEV * narrow_count
    slot_ids = jnp.full((buffer_rows,), -1, jnp.int32).at[position].set(pair_slot)
    source_row = jnp.zeros((buffer_rows,), jnp.int32).at[position].set(
        jnp.arange(pair_rows, dtype=jnp.int32)
    )
    filled = jnp.zeros((buffer_rows,), jnp.bool_).at[position].set(True)
    send_buffer = jnp.where(filled[:, None, None], quarters[source_row], 0.0)
    received = lax.all_to_all(send_buffer, "wide", split_axis=0, concat_axis=0, tiled=True)
    got_slots = lax.all_to_all(slot_ids, "wide", split_axis=0, concat_axis=0, tiled=True)
    slot_table = (got_slots[:, None] == jnp.arange(row_slots, dtype=jnp.int32)[None, :]).astype(
        jnp.float32
    )
    slot_sums = jnp.einsum("ri,rab->iab", slot_table, received, precision=lax.Precision.HIGHEST)
    slot_sums = slot_sums.reshape(narrow_count, T_DEV, quarter_rows, B)
    summed = lax.all_to_all(slot_sums, "narrow", split_axis=0, concat_axis=2, tiled=True)
    summed = summed.reshape(T_DEV, B, B)
    return (factor_back, lower_back, ancestor - summed)


def solution(mesh):
    placed = (
        P("wide", None, "narrow"),
        P("wide", None, "narrow"),
        P("wide"),
        P("wide", None),
        P("wide"),
        P(("wide", "narrow"), None, None),
    )
    return jax.shard_map(
        local,
        mesh=mesh,
        in_specs=placed,
        out_specs=(
            P("wide", None, "narrow"),
            P("wide", None, "narrow"),
            P(("wide", "narrow"), None, None),
        ),
        check_vma=False,
    )
```

```python
import functools

import jax
import jax.numpy as jnp
import numpy as np
from jax import lax
from jax.experimental import pallas as pl
from jax.experimental.pallas import tpu as pltpu
from jax.sharding import PartitionSpec as P

MESH = pl.DeviceIdType.MESH

W = 512
B = 128
P_SIZE = 8
T_DEV = 2


def pair_lists(count):
    first = []
    second = []
    for outer in range(count):
        for inner in range(outer + 1):
            first.append(outer)
            second.append(inner)
    return (np.array(first, np.int32), np.array(second, np.int32))


def columns_out_kernel(x_ref, y_ref, send_sem, recv_sem, own_sem, *, count, group, width):
    me = lax.axis_index("narrow")
    wide = lax.axis_index("wide")
    barrier = pltpu.get_barrier_semaphore()
    for d in range(1, count):
        peer = lax.rem(me + d, count)
        pl.semaphore_signal(barrier, inc=1, device_id=(wide, peer), device_id_type=MESH)
    pl.semaphore_wait(barrier, count - 1)
    mine = y_ref.at[pl.ds(me * group, group)]
    own = pltpu.make_async_copy(
        x_ref.at[:, :, pl.ds(pl.multiple_of(me * width, width), width)], mine, own_sem
    )
    own.start()
    copies = []
    for d in range(1, count):
        peer = lax.rem(me + d, count)
        copy = pltpu.make_async_remote_copy(
            src_ref=x_ref.at[:, :, pl.ds(pl.multiple_of(peer * width, width), width)],
            dst_ref=mine,
            send_sem=send_sem.at[d - 1],
            recv_sem=recv_sem.at[d - 1],
            device_id=(wide, peer),
            device_id_type=MESH,
        )
        copy.start()
        copies.append(copy)
    own.wait()
    for copy in copies:
        copy.wait()


def columns_out(x, count, width, collective_id):
    group, rows, _ = x.shape
    nbytes = x.size * 4
    return pl.pallas_call(
        functools.partial(columns_out_kernel, count=count, group=group, width=width),
        out_shape=jax.ShapeDtypeStruct((group * count, rows, width), x.dtype),
        in_specs=[pl.BlockSpec(memory_space=pl.ANY)],
        out_specs=pl.BlockSpec(memory_space=pl.ANY),
        scratch_shapes=[
            pltpu.SemaphoreType.DMA((count - 1,)),
            pltpu.SemaphoreType.DMA((count - 1,)),
            pltpu.SemaphoreType.DMA,
        ],
        compiler_params=pltpu.CompilerParams(collective_id=collective_id, has_side_effects=True),
        cost_estimate=pl.CostEstimate(flops=0, bytes_accessed=2 * nbytes, transcendentals=0),
    )(x)


def mm(a, b):
    return jnp.einsum("sik,skj->sij", a, b, precision=lax.Precision.HIGHEST)


def mm_t(a, b):
    return jnp.einsum("sik,sjk->sij", a, b, precision=lax.Precision.HIGHEST)


def blocked_cholesky(matrix):
    batch, size, _ = matrix.shape
    nblk = size // B
    eye = jnp.broadcast_to(jnp.eye(B, dtype=jnp.float32), (batch, B, B))
    trailing = matrix
    diag_l, diag_inv, below = [], [], []
    inverse_rows = []
    for k in range(nblk):
        head = trailing[:, :B, :B]
        l_kk = lax.linalg.cholesky(head, symmetrize_input=False)
        i_kk = lax.linalg.triangular_solve(l_kk, eye, left_side=True, lower=True)
        diag_l.append(l_kk)
        diag_inv.append(i_kk)
        if k > 0:
            left = jnp.concatenate([below[j][:, (k - j - 1) * B:(k - j) * B, :] for j in range(k)], axis=2)
            upper = jnp.concatenate(inverse_rows, axis=1)
            rest = -mm(left, upper)
            rest = jnp.concatenate([rest[:, :, :k * B], eye, rest[:, :, (k + 1) * B:]], axis=2)
            inverse_rows.append(mm(i_kk, rest))
        else:
            inverse_rows.append(jnp.concatenate(
                [i_kk, jnp.zeros((batch, B, size - B), jnp.float32)], axis=2))
        if k < nblk - 1:
            panel_k = mm_t(trailing[:, B:, :B], i_kk)
            below.append(panel_k)
            trailing = trailing[:, B:, B:] - mm_t(panel_k, panel_k)
    columns = []
    for k in range(nblk):
        parts = []
        if k > 0:
            parts.append(jnp.zeros((batch, k * B, B), jnp.float32))
        parts.append(diag_l[k])
        if k < nblk - 1:
            parts.append(below[k])
        columns.append(jnp.concatenate(parts, axis=1))
    factor = jnp.concatenate(columns, axis=2)
    inverse = jnp.concatenate(inverse_rows, axis=1)
    return factor, inverse


def local(diag_block, panel, panel_count, pair_owner, pair_slot, ancestor):
    supers_here = diag_block.shape[0]
    col_width = diag_block.shape[2]
    diag_rows = diag_block.shape[1]
    narrow_index = lax.axis_index("narrow")
    narrow_count = lax.axis_size("narrow")
    wide_count = lax.axis_size("wide")
    group = supers_here // narrow_count

    whole_diag = lax.all_to_all(diag_block, "narrow", split_axis=0, concat_axis=2, tiled=True)
    whole_panel = lax.all_to_all(panel, "narrow", split_axis=0, concat_axis=2, tiled=True)

    factor, inverse = blocked_cholesky(whole_diag)
    lower_panel = jnp.einsum(
        "srk,sck->src", whole_panel, inverse, precision=lax.Precision.HIGHEST
    )
    counts = lax.dynamic_slice_in_dim(panel_count, narrow_index * group, group)
    block_index = jnp.arange(P_SIZE * B, dtype=jnp.int32) // B
    live = (block_index[None, :] < counts[:, None]).astype(jnp.float32)
    lower_panel = lower_panel * live[:, :, None]

    first, second = pair_lists(P_SIZE)
    npair = len(first)
    blocks = lower_panel.reshape(group, P_SIZE, B, W)
    contribution = jnp.einsum(
        "spac,spbc->spab", blocks[:, first], blocks[:, second], precision=lax.Precision.HIGHEST
    )

    quarters = lax.all_to_all(contribution, "narrow", split_axis=2, concat_axis=0, tiled=True)
    quarter_rows = quarters.shape[2]
    pair_rows = supers_here * npair
    quarters = quarters.reshape(pair_rows, quarter_rows, B)

    capacity = max(2, (pair_rows + wide_count - 1) // wide_count)
    owners = pair_owner[:, 0]
    owner_table = (owners[:, None] == jnp.arange(wide_count, dtype=jnp.int32)[None, :]).astype(
        jnp.int32
    )
    earlier = jnp.cumsum(owner_table, axis=0) - owner_table
    rank_here = jnp.sum(earlier * owner_table, axis=1)
    position = owners * capacity + rank_here
    buffer_rows = wide_count * capacity
    row_slots = T_DEV * narrow_count
    slot_ids = jnp.full((buffer_rows,), -1, jnp.int32).at[position].set(pair_slot)
    source_row = jnp.zeros((buffer_rows,), jnp.int32).at[position].set(
        jnp.arange(pair_rows, dtype=jnp.int32)
    )
    filled = jnp.zeros((buffer_rows,), jnp.bool_).at[position].set(True)
    send_buffer = jnp.where(filled[:, None, None], quarters[source_row], 0.0)
    send_buffer, factor, lower_panel = lax.optimization_barrier((send_buffer, factor, lower_panel))
    received = lax.all_to_all(send_buffer, "wide", split_axis=0, concat_axis=0, tiled=True)
    factor_back = columns_out(factor, narrow_count, col_width, 0)
    lower_back = columns_out(lower_panel, narrow_count, col_width, 1)
    received, factor_back, lower_back = lax.optimization_barrier((received, factor_back, lower_back))
    got_slots = lax.all_to_all(slot_ids, "wide", split_axis=0, concat_axis=0, tiled=True)
    slot_table = (got_slots[:, None] == jnp.arange(row_slots, dtype=jnp.int32)[None, :]).astype(
        jnp.float32
    )
    slot_sums = jnp.einsum("ri,rab->iab", slot_table, received, precision=lax.Precision.HIGHEST)
    slot_sums = slot_sums.reshape(narrow_count, T_DEV, quarter_rows, B)
    summed = lax.all_to_all(slot_sums, "narrow", split_axis=0, concat_axis=2, tiled=True)
    summed = summed.reshape(T_DEV, B, B)
    return (factor_back, lower_back, ancestor - summed)


def solution(mesh):
    placed = (
        P("wide", None, "narrow"),
        P("wide", None, "narrow"),
        P("wide"),
        P("wide", None),
        P("wide"),
        P(("wide", "narrow"), None, None),
    )
    return jax.shard_map(
        local,
        mesh=mesh,
        in_specs=placed,
        out_specs=(
            P("wide", None, "narrow"),
            P("wide", None, "narrow"),
            P(("wide", "narrow"), None, None),
        ),
        check_vma=False,
    )
```

```python
import functools

import jax
import jax.numpy as jnp
import numpy as np
from jax import lax
from jax.experimental import pallas as pl
from jax.experimental.pallas import tpu as pltpu
from jax.sharding import PartitionSpec as P

MESH = pl.DeviceIdType.MESH

W = 512
B = 128
P_SIZE = 8
T_DEV = 2


def pair_lists(count):
    first = []
    second = []
    for outer in range(count):
        for inner in range(outer + 1):
            first.append(outer)
            second.append(inner)
    return (np.array(first, np.int32), np.array(second, np.int32))


def columns_out_kernel(x_ref, y_ref, send_sem, recv_sem, own_sem, *, count, group, width):
    me = lax.axis_index("narrow")
    wide = lax.axis_index("wide")
    barrier = pltpu.get_barrier_semaphore()
    for d in range(1, count):
        peer = lax.rem(me + d, count)
        pl.semaphore_signal(barrier, inc=1, device_id=(wide, peer), device_id_type=MESH)
    pl.semaphore_wait(barrier, count - 1)
    mine = y_ref.at[pl.ds(me * group, group)]
    own = pltpu.make_async_copy(
        x_ref.at[:, :, pl.ds(pl.multiple_of(me * width, width), width)], mine, own_sem
    )
    own.start()
    copies = []
    for d in range(1, count):
        peer = lax.rem(me + d, count)
        copy = pltpu.make_async_remote_copy(
            src_ref=x_ref.at[:, :, pl.ds(pl.multiple_of(peer * width, width), width)],
            dst_ref=mine,
            send_sem=send_sem.at[d - 1],
            recv_sem=recv_sem.at[d - 1],
            device_id=(wide, peer),
            device_id_type=MESH,
        )
        copy.start()
        copies.append(copy)
    own.wait()
    for copy in copies:
        copy.wait()


def columns_out(x, count, width, collective_id):
    group, rows, _ = x.shape
    nbytes = x.size * 4
    return pl.pallas_call(
        functools.partial(columns_out_kernel, count=count, group=group, width=width),
        out_shape=jax.ShapeDtypeStruct((group * count, rows, width), x.dtype),
        in_specs=[pl.BlockSpec(memory_space=pl.ANY)],
        out_specs=pl.BlockSpec(memory_space=pl.ANY),
        scratch_shapes=[
            pltpu.SemaphoreType.DMA((count - 1,)),
            pltpu.SemaphoreType.DMA((count - 1,)),
            pltpu.SemaphoreType.DMA,
        ],
        compiler_params=pltpu.CompilerParams(collective_id=collective_id, has_side_effects=True),
        cost_estimate=pl.CostEstimate(flops=0, bytes_accessed=2 * nbytes, transcendentals=0),
    )(x)


def mm(a, b):
    return jnp.einsum("sik,skj->sij", a, b, precision=lax.Precision.HIGHEST)


def mm_t(a, b):
    return jnp.einsum("sik,sjk->sij", a, b, precision=lax.Precision.HIGHEST)


def blocked_cholesky(matrix):
    batch, size, _ = matrix.shape
    nblk = size // B
    eye = jnp.broadcast_to(jnp.eye(B, dtype=jnp.float32), (batch, B, B))
    trailing = matrix
    diag_l, diag_inv, below = [], [], []
    inverse_rows = []
    for k in range(nblk):
        head = trailing[:, :B, :B]
        l_kk = lax.linalg.cholesky(head, symmetrize_input=False)
        i_kk = lax.linalg.triangular_solve(l_kk, eye, left_side=True, lower=True)
        diag_l.append(l_kk)
        diag_inv.append(i_kk)
        if k > 0:
            left = jnp.concatenate([below[j][:, (k - j - 1) * B:(k - j) * B, :] for j in range(k)], axis=2)
            upper = jnp.concatenate(inverse_rows, axis=1)
            rest = -mm(left, upper)
            rest = jnp.concatenate([rest[:, :, :k * B], eye, rest[:, :, (k + 1) * B:]], axis=2)
            inverse_rows.append(mm(i_kk, rest))
        else:
            inverse_rows.append(jnp.concatenate(
                [i_kk, jnp.zeros((batch, B, size - B), jnp.float32)], axis=2))
        if k < nblk - 1:
            panel_k = mm_t(trailing[:, B:, :B], i_kk)
            below.append(panel_k)
            trailing = trailing[:, B:, B:] - mm_t(panel_k, panel_k)
    columns = []
    for k in range(nblk):
        parts = []
        if k > 0:
            parts.append(jnp.zeros((batch, k * B, B), jnp.float32))
        parts.append(diag_l[k])
        if k < nblk - 1:
            parts.append(below[k])
        columns.append(jnp.concatenate(parts, axis=1))
    factor = jnp.concatenate(columns, axis=2)
    inverse = jnp.concatenate(inverse_rows, axis=1)
    return factor, inverse


def local(diag_block, panel, panel_count, pair_owner, pair_slot, ancestor):
    supers_here = diag_block.shape[0]
    col_width = diag_block.shape[2]
    diag_rows = diag_block.shape[1]
    narrow_index = lax.axis_index("narrow")
    narrow_count = lax.axis_size("narrow")
    wide_count = lax.axis_size("wide")
    group = supers_here // narrow_count

    whole_diag = lax.all_to_all(diag_block, "narrow", split_axis=0, concat_axis=2, tiled=True)
    whole_panel = lax.all_to_all(panel, "narrow", split_axis=0, concat_axis=2, tiled=True)

    factor, inverse = blocked_cholesky(whole_diag)
    lower_panel = jnp.einsum(
        "srk,sck->src", whole_panel, inverse, precision=lax.Precision.HIGHEST
    )
    counts = lax.dynamic_slice_in_dim(panel_count, narrow_index * group, group)
    block_index = jnp.arange(P_SIZE * B, dtype=jnp.int32) // B
    live = (block_index[None, :] < counts[:, None]).astype(jnp.float32)
    lower_panel = lower_panel * live[:, :, None]

    first, second = pair_lists(P_SIZE)
    npair = len(first)
    blocks = lower_panel.reshape(group, P_SIZE, B, W)
    gram = jnp.einsum("siac,sjbc->sijab", blocks, blocks, precision=lax.Precision.HIGHEST)
    gram = gram.reshape(group, P_SIZE * P_SIZE, B, B)
    contribution = gram[:, first * P_SIZE + second]

    quarters = lax.all_to_all(contribution, "narrow", split_axis=2, concat_axis=0, tiled=True)
    quarter_rows = quarters.shape[2]
    pair_rows = supers_here * npair
    quarters = quarters.reshape(pair_rows, quarter_rows, B)

    capacity = max(2, (pair_rows + wide_count - 1) // wide_count)
    owners = pair_owner[:, 0]
    owner_table = (owners[:, None] == jnp.arange(wide_count, dtype=jnp.int32)[None, :]).astype(
        jnp.int32
    )
    earlier = jnp.cumsum(owner_table, axis=0) - owner_table
    rank_here = jnp.sum(earlier * owner_table, axis=1)
    position = owners * capacity + rank_here
    buffer_rows = wide_count * capacity
    row_slots = T_DEV * narrow_count
    slot_ids = jnp.full((buffer_rows,), -1.0, jnp.float32).at[position].set(
        pair_slot.astype(jnp.float32)
    )
    source_row = jnp.zeros((buffer_rows,), jnp.int32).at[position].set(
        jnp.arange(pair_rows, dtype=jnp.int32)
    )
    filled = jnp.zeros((buffer_rows,), jnp.bool_).at[position].set(True)
    send_buffer = jnp.where(filled[:, None, None], quarters[source_row], 0.0)
    meta = jnp.zeros((wide_count, 8, B), jnp.float32)
    meta = meta.at[:, 0, :capacity].set(slot_ids.reshape(wide_count, capacity))
    send_buffer = jnp.concatenate(
        [send_buffer.reshape(wide_count, capacity * quarter_rows, B), meta], axis=1
    )
    send_buffer, factor, lower_panel = lax.optimization_barrier((send_buffer, factor, lower_panel))
    received = lax.all_to_all(send_buffer, "wide", split_axis=0, concat_axis=0, tiled=True)
    factor_back = columns_out(factor, narrow_count, col_width, 0)
    lower_back = columns_out(lower_panel, narrow_count, col_width, 1)
    received, factor_back, lower_back = lax.optimization_barrier((received, factor_back, lower_back))
    got_slots = received[:, capacity * quarter_rows, :capacity].reshape(buffer_rows)
    got_slots = got_slots.astype(jnp.int32)
    received = received[:, : capacity * quarter_rows, :].reshape(buffer_rows, quarter_rows, B)
    slot_table = (got_slots[:, None] == jnp.arange(row_slots, dtype=jnp.int32)[None, :]).astype(
        jnp.float32
    )
    slot_sums = jnp.einsum("ri,rab->iab", slot_table, received, precision=lax.Precision.HIGHEST)
    slot_sums = slot_sums.reshape(narrow_count, T_DEV, quarter_rows, B)
    summed = lax.all_to_all(slot_sums, "narrow", split_axis=0, concat_axis=2, tiled=True)
    summed = summed.reshape(T_DEV, B, B)
    return (factor_back, lower_back, ancestor - summed)


def solution(mesh):
    placed = (
        P("wide", None, "narrow"),
        P("wide", None, "narrow"),
        P("wide"),
        P("wide", None),
        P("wide"),
        P(("wide", "narrow"), None, None),
    )
    return jax.shard_map(
        local,
        mesh=mesh,
        in_specs=placed,
        out_specs=(
            P("wide", None, "narrow"),
            P("wide", None, "narrow"),
            P(("wide", "narrow"), None, None),
        ),
        check_vma=False,
    )
```

```python
import functools

import jax
import jax.numpy as jnp
import numpy as np
from jax import lax
from jax.experimental import pallas as pl
from jax.experimental.pallas import tpu as pltpu
from jax.sharding import PartitionSpec as P

MESH = pl.DeviceIdType.MESH

W = 512
B = 128
P_SIZE = 8
T_DEV = 2


def pair_lists(count):
    first = []
    second = []
    for outer in range(count):
        for inner in range(outer + 1):
            first.append(outer)
            second.append(inner)
    return (np.array(first, np.int32), np.array(second, np.int32))


def columns_out_kernel(x_ref, y_ref, send_sem, recv_sem, own_sem, *, count, group, width):
    me = lax.axis_index("narrow")
    wide = lax.axis_index("wide")
    barrier = pltpu.get_barrier_semaphore()
    for d in range(1, count):
        peer = lax.rem(me + d, count)
        pl.semaphore_signal(barrier, inc=1, device_id=(wide, peer), device_id_type=MESH)
    pl.semaphore_wait(barrier, count - 1)
    mine = y_ref.at[pl.ds(me * group, group)]
    own = pltpu.make_async_copy(
        x_ref.at[:, :, pl.ds(pl.multiple_of(me * width, width), width)], mine, own_sem
    )
    own.start()
    copies = []
    for d in range(1, count):
        peer = lax.rem(me + d, count)
        copy = pltpu.make_async_remote_copy(
            src_ref=x_ref.at[:, :, pl.ds(pl.multiple_of(peer * width, width), width)],
            dst_ref=mine,
            send_sem=send_sem.at[d - 1],
            recv_sem=recv_sem.at[d - 1],
            device_id=(wide, peer),
            device_id_type=MESH,
        )
        copy.start()
        copies.append(copy)
    own.wait()
    for copy in copies:
        copy.wait()


def columns_out(x, count, width, collective_id):
    group, rows, _ = x.shape
    nbytes = x.size * 4
    return pl.pallas_call(
        functools.partial(columns_out_kernel, count=count, group=group, width=width),
        out_shape=jax.ShapeDtypeStruct((group * count, rows, width), x.dtype),
        in_specs=[pl.BlockSpec(memory_space=pl.ANY)],
        out_specs=pl.BlockSpec(memory_space=pl.ANY),
        scratch_shapes=[
            pltpu.SemaphoreType.DMA((count - 1,)),
            pltpu.SemaphoreType.DMA((count - 1,)),
            pltpu.SemaphoreType.DMA,
        ],
        compiler_params=pltpu.CompilerParams(collective_id=collective_id, has_side_effects=True),
        cost_estimate=pl.CostEstimate(flops=0, bytes_accessed=2 * nbytes, transcendentals=0),
    )(x)


def block_chol_kernel(a_ref, l_ref, inv_ref, work, upper, elim):
    n = a_ref.shape[0]
    work[...] = a_ref[...]
    rows = lax.broadcasted_iota(jnp.int32, (n, n), 0)
    cols = lax.broadcasted_iota(jnp.int32, (n, n), 1)
    elim[...] = (rows == cols).astype(jnp.float32)
    lane = lax.broadcasted_iota(jnp.int32, (1, n), 1)
    row_id = lax.broadcasted_iota(jnp.int32, (n, 1), 0)

    def step(j, carry):
        r = work[pl.ds(j, 1), :]
        piv = jnp.sum(jnp.where(lane == j, r, 0.0), axis=1, keepdims=True)
        root = jnp.sqrt(piv)
        scale = 1.0 / root
        u_row = jnp.where(lane >= j, r * scale, 0.0)
        upper[pl.ds(j, 1), :] = u_row
        e_row = elim[pl.ds(j, 1), :]
        inv_ref[pl.ds(j, 1), :] = e_row * scale
        u_col = jnp.transpose(jnp.broadcast_to(u_row, (8, n)))[:, 0:1]
        work[...] = work[...] - u_col * u_row
        mult = jnp.where(row_id > j, u_col * scale, 0.0)
        elim[...] = elim[...] - mult * e_row
        return carry

    lax.fori_loop(0, n, step, 0)
    l_ref[...] = jnp.transpose(upper[...])


def block_chol(a):
    n = a.shape[-1]
    return pl.pallas_call(
        block_chol_kernel,
        out_shape=(jax.ShapeDtypeStruct((n, n), jnp.float32), jax.ShapeDtypeStruct((n, n), jnp.float32)),
        in_specs=[pl.BlockSpec(memory_space=pltpu.VMEM)],
        out_specs=(pl.BlockSpec(memory_space=pltpu.VMEM), pl.BlockSpec(memory_space=pltpu.VMEM)),
        scratch_shapes=[pltpu.VMEM((n, n), jnp.float32)] * 3,
    )(a)


def mm(a, b):
    return jnp.einsum("sik,skj->sij", a, b, precision=lax.Precision.HIGHEST)


def mm_t(a, b):
    return jnp.einsum("sik,sjk->sij", a, b, precision=lax.Precision.HIGHEST)


def blocked_cholesky(matrix):
    batch, size, _ = matrix.shape
    nblk = size // B
    eye = jnp.broadcast_to(jnp.eye(B, dtype=jnp.float32), (batch, B, B))
    trailing = matrix
    diag_l, diag_inv, below = [], [], []
    inverse_rows = []
    for k in range(nblk):
        head = trailing[:, :B, :B]
        pieces = [block_chol(head[b]) for b in range(batch)]
        l_kk = jnp.stack([p[0] for p in pieces])
        i_kk = jnp.stack([p[1] for p in pieces])
        diag_l.append(l_kk)
        diag_inv.append(i_kk)
        if k > 0:
            left = jnp.concatenate([below[j][:, (k - j - 1) * B:(k - j) * B, :] for j in range(k)], axis=2)
            upper = jnp.concatenate(inverse_rows, axis=1)
            rest = -mm(left, upper)
            rest = jnp.concatenate([rest[:, :, :k * B], eye, rest[:, :, (k + 1) * B:]], axis=2)
            inverse_rows.append(mm(i_kk, rest))
        else:
            inverse_rows.append(jnp.concatenate(
                [i_kk, jnp.zeros((batch, B, size - B), jnp.float32)], axis=2))
        if k < nblk - 1:
            panel_k = mm_t(trailing[:, B:, :B], i_kk)
            below.append(panel_k)
            trailing = trailing[:, B:, B:] - mm_t(panel_k, panel_k)
    columns = []
    for k in range(nblk):
        parts = []
        if k > 0:
            parts.append(jnp.zeros((batch, k * B, B), jnp.float32))
        parts.append(diag_l[k])
        if k < nblk - 1:
            parts.append(below[k])
        columns.append(jnp.concatenate(parts, axis=1))
    factor = jnp.concatenate(columns, axis=2)
    inverse = jnp.concatenate(inverse_rows, axis=1)
    return factor, inverse


def local(diag_block, panel, panel_count, pair_owner, pair_slot, ancestor):
    supers_here = diag_block.shape[0]
    col_width = diag_block.shape[2]
    diag_rows = diag_block.shape[1]
    narrow_index = lax.axis_index("narrow")
    narrow_count = lax.axis_size("narrow")
    wide_count = lax.axis_size("wide")
    group = supers_here // narrow_count

    whole_diag = lax.all_to_all(diag_block, "narrow", split_axis=0, concat_axis=2, tiled=True)
    whole_panel = lax.all_to_all(panel, "narrow", split_axis=0, concat_axis=2, tiled=True)

    factor, inverse = blocked_cholesky(whole_diag)
    lower_panel = jnp.einsum(
        "srk,sck->src", whole_panel, inverse, precision=lax.Precision.HIGHEST
    )
    counts = lax.dynamic_slice_in_dim(panel_count, narrow_index * group, group)
    block_index = jnp.arange(P_SIZE * B, dtype=jnp.int32) // B
    live = (block_index[None, :] < counts[:, None]).astype(jnp.float32)
    lower_panel = lower_panel * live[:, :, None]

    first, second = pair_lists(P_SIZE)
    npair = len(first)
    blocks = lower_panel.reshape(group, P_SIZE, B, W)
    gram = jnp.einsum("siac,sjbc->sijab", blocks, blocks, precision=lax.Precision.HIGHEST)
    gram = gram.reshape(group, P_SIZE * P_SIZE, B, B)
    contribution = gram[:, first * P_SIZE + second]

    quarters = lax.all_to_all(contribution, "narrow", split_axis=2, concat_axis=0, tiled=True)
    quarter_rows = quarters.shape[2]
    pair_rows = supers_here * npair
    quarters = quarters.reshape(pair_rows, quarter_rows, B)

    capacity = max(2, (pair_rows + wide_count - 1) // wide_count)
    owners = pair_owner[:, 0]
    owner_table = (owners[:, None] == jnp.arange(wide_count, dtype=jnp.int32)[None, :]).astype(
        jnp.int32
    )
    earlier = jnp.cumsum(owner_table, axis=0) - owner_table
    rank_here = jnp.sum(earlier * owner_table, axis=1)
    position = owners * capacity + rank_here
    buffer_rows = wide_count * capacity
    row_slots = T_DEV * narrow_count
    slot_ids = jnp.full((buffer_rows,), -1.0, jnp.float32).at[position].set(
        pair_slot.astype(jnp.float32)
    )
    source_row = jnp.zeros((buffer_rows,), jnp.int32).at[position].set(
        jnp.arange(pair_rows, dtype=jnp.int32)
    )
    filled = jnp.zeros((buffer_rows,), jnp.bool_).at[position].set(True)
    send_buffer = jnp.where(filled[:, None, None], quarters[source_row], 0.0)
    meta = jnp.zeros((wide_count, 8, B), jnp.float32)
    meta = meta.at[:, 0, :capacity].set(slot_ids.reshape(wide_count, capacity))
    send_buffer = jnp.concatenate(
        [send_buffer.reshape(wide_count, capacity * quarter_rows, B), meta], axis=1
    )
    send_buffer, factor, lower_panel = lax.optimization_barrier((send_buffer, factor, lower_panel))
    received = lax.all_to_all(send_buffer, "wide", split_axis=0, concat_axis=0, tiled=True)
    factor_back = columns_out(factor, narrow_count, col_width, 0)
    lower_back = columns_out(lower_panel, narrow_count, col_width, 1)
    received, factor_back, lower_back = lax.optimization_barrier((received, factor_back, lower_back))
    got_slots = received[:, capacity * quarter_rows, :capacity].reshape(buffer_rows)
    got_slots = got_slots.astype(jnp.int32)
    received = received[:, : capacity * quarter_rows, :].reshape(buffer_rows, quarter_rows, B)
    slot_table = (got_slots[:, None] == jnp.arange(row_slots, dtype=jnp.int32)[None, :]).astype(
        jnp.float32
    )
    slot_sums = jnp.einsum("ri,rab->iab", slot_table, received, precision=lax.Precision.HIGHEST)
    slot_sums = slot_sums.reshape(narrow_count, T_DEV, quarter_rows, B)
    summed = lax.all_to_all(slot_sums, "narrow", split_axis=0, concat_axis=2, tiled=True)
    summed = summed.reshape(T_DEV, B, B)
    return (factor_back, lower_back, ancestor - summed)


def solution(mesh):
    placed = (
        P("wide", None, "narrow"),
        P("wide", None, "narrow"),
        P("wide"),
        P("wide", None),
        P("wide"),
        P(("wide", "narrow"), None, None),
    )
    return jax.shard_map(
        local,
        mesh=mesh,
        in_specs=placed,
        out_specs=(
            P("wide", None, "narrow"),
            P("wide", None, "narrow"),
            P(("wide", "narrow"), None, None),
        ),
        check_vma=False,
    )
```

```python
import functools

import jax
import jax.numpy as jnp
import numpy as np
from jax import lax
from jax.experimental import pallas as pl
from jax.experimental.pallas import tpu as pltpu
from jax.sharding import PartitionSpec as P

MESH = pl.DeviceIdType.MESH

W = 512
B = 128
P_SIZE = 8
T_DEV = 2


def pair_lists(count):
    first = []
    second = []
    for outer in range(count):
        for inner in range(outer + 1):
            first.append(outer)
            second.append(inner)
    return (np.array(first, np.int32), np.array(second, np.int32))


def columns_out_kernel(x_ref, y_ref, send_sem, recv_sem, own_sem, *, count, group, width):
    me = lax.axis_index("narrow")
    wide = lax.axis_index("wide")
    barrier = pltpu.get_barrier_semaphore()
    for d in range(1, count):
        peer = lax.rem(me + d, count)
        pl.semaphore_signal(barrier, inc=1, device_id=(wide, peer), device_id_type=MESH)
    pl.semaphore_wait(barrier, count - 1)
    mine = y_ref.at[pl.ds(me * group, group)]
    own = pltpu.make_async_copy(
        x_ref.at[:, :, pl.ds(pl.multiple_of(me * width, width), width)], mine, own_sem
    )
    own.start()
    copies = []
    for d in range(1, count):
        peer = lax.rem(me + d, count)
        copy = pltpu.make_async_remote_copy(
            src_ref=x_ref.at[:, :, pl.ds(pl.multiple_of(peer * width, width), width)],
            dst_ref=mine,
            send_sem=send_sem.at[d - 1],
            recv_sem=recv_sem.at[d - 1],
            device_id=(wide, peer),
            device_id_type=MESH,
        )
        copy.start()
        copies.append(copy)
    own.wait()
    for copy in copies:
        copy.wait()


def columns_out(x, count, width, collective_id):
    group, rows, _ = x.shape
    nbytes = x.size * 4
    return pl.pallas_call(
        functools.partial(columns_out_kernel, count=count, group=group, width=width),
        out_shape=jax.ShapeDtypeStruct((group * count, rows, width), x.dtype),
        in_specs=[pl.BlockSpec(memory_space=pl.ANY)],
        out_specs=pl.BlockSpec(memory_space=pl.ANY),
        scratch_shapes=[
            pltpu.SemaphoreType.DMA((count - 1,)),
            pltpu.SemaphoreType.DMA((count - 1,)),
            pltpu.SemaphoreType.DMA,
        ],
        compiler_params=pltpu.CompilerParams(collective_id=collective_id, has_side_effects=True),
        cost_estimate=pl.CostEstimate(flops=0, bytes_accessed=2 * nbytes, transcendentals=0),
    )(x)


def block_chol_kernel(a_ref, l_ref, inv_ref, work, upper, elim):
    n = a_ref.shape[0]
    work[...] = a_ref[...]
    rows = lax.broadcasted_iota(jnp.int32, (n, n), 0)
    cols = lax.broadcasted_iota(jnp.int32, (n, n), 1)
    elim[...] = (rows == cols).astype(jnp.float32)
    lane = lax.broadcasted_iota(jnp.int32, (1, n), 1)
    row_id = lax.broadcasted_iota(jnp.int32, (n, 1), 0)

    def step(j, carry):
        r = work[pl.ds(j, 1), :]
        piv = jnp.sum(jnp.where(lane == j, r, 0.0), axis=1, keepdims=True)
        root = jnp.sqrt(piv)
        scale = 1.0 / root
        u_row = jnp.where(lane >= j, r * scale, 0.0)
        upper[pl.ds(j, 1), :] = u_row
        e_row = elim[pl.ds(j, 1), :]
        inv_ref[pl.ds(j, 1), :] = e_row * scale
        whole = work[...]
        u_col = jnp.sum(jnp.where(cols == j, whole, 0.0), axis=1, keepdims=True) * scale
        u_col = jnp.where(row_id >= j, u_col, 0.0)
        work[...] = whole - u_col * u_row
        mult = jnp.where(row_id > j, u_col * scale, 0.0)
        elim[...] = elim[...] - mult * e_row
        return carry

    lax.fori_loop(0, n, step, 0)
    l_ref[...] = jnp.transpose(upper[...])


def block_chol(a):
    n = a.shape[-1]
    return pl.pallas_call(
        block_chol_kernel,
        out_shape=(jax.ShapeDtypeStruct((n, n), jnp.float32), jax.ShapeDtypeStruct((n, n), jnp.float32)),
        in_specs=[pl.BlockSpec(memory_space=pltpu.VMEM)],
        out_specs=(pl.BlockSpec(memory_space=pltpu.VMEM), pl.BlockSpec(memory_space=pltpu.VMEM)),
        scratch_shapes=[pltpu.VMEM((n, n), jnp.float32)] * 3,
    )(a)


def mm(a, b):
    return jnp.einsum("sik,skj->sij", a, b, precision=lax.Precision.HIGHEST)


def mm_t(a, b):
    return jnp.einsum("sik,sjk->sij", a, b, precision=lax.Precision.HIGHEST)


def blocked_cholesky(matrix):
    batch, size, _ = matrix.shape
    nblk = size // B
    eye = jnp.broadcast_to(jnp.eye(B, dtype=jnp.float32), (batch, B, B))
    trailing = matrix
    diag_l, diag_inv, below = [], [], []
    inverse_rows = []
    for k in range(nblk):
        head = trailing[:, :B, :B]
        pieces = [block_chol(head[b]) for b in range(batch)]
        l_kk = jnp.stack([p[0] for p in pieces])
        i_kk = jnp.stack([p[1] for p in pieces])
        diag_l.append(l_kk)
        diag_inv.append(i_kk)
        if k > 0:
            left = jnp.concatenate([below[j][:, (k - j - 1) * B:(k - j) * B, :] for j in range(k)], axis=2)
            upper = jnp.concatenate(inverse_rows, axis=1)
            rest = -mm(left, upper)
            rest = jnp.concatenate([rest[:, :, :k * B], eye, rest[:, :, (k + 1) * B:]], axis=2)
            inverse_rows.append(mm(i_kk, rest))
        else:
            inverse_rows.append(jnp.concatenate(
                [i_kk, jnp.zeros((batch, B, size - B), jnp.float32)], axis=2))
        if k < nblk - 1:
            panel_k = mm_t(trailing[:, B:, :B], i_kk)
            below.append(panel_k)
            trailing = trailing[:, B:, B:] - mm_t(panel_k, panel_k)
    columns = []
    for k in range(nblk):
        parts = []
        if k > 0:
            parts.append(jnp.zeros((batch, k * B, B), jnp.float32))
        parts.append(diag_l[k])
        if k < nblk - 1:
            parts.append(below[k])
        columns.append(jnp.concatenate(parts, axis=1))
    factor = jnp.concatenate(columns, axis=2)
    inverse = jnp.concatenate(inverse_rows, axis=1)
    return factor, inverse


def local(diag_block, panel, panel_count, pair_owner, pair_slot, ancestor):
    supers_here = diag_block.shape[0]
    col_width = diag_block.shape[2]
    diag_rows = diag_block.shape[1]
    narrow_index = lax.axis_index("narrow")
    narrow_count = lax.axis_size("narrow")
    wide_count = lax.axis_size("wide")
    group = supers_here // narrow_count

    whole_diag = lax.all_to_all(diag_block, "narrow", split_axis=0, concat_axis=2, tiled=True)
    whole_panel = lax.all_to_all(panel, "narrow", split_axis=0, concat_axis=2, tiled=True)

    factor, inverse = blocked_cholesky(whole_diag)
    lower_panel = jnp.einsum(
        "srk,sck->src", whole_panel, inverse, precision=lax.Precision.HIGHEST
    )
    counts = lax.dynamic_slice_in_dim(panel_count, narrow_index * group, group)
    block_index = jnp.arange(P_SIZE * B, dtype=jnp.int32) // B
    live = (block_index[None, :] < counts[:, None]).astype(jnp.float32)
    lower_panel = lower_panel * live[:, :, None]

    first, second = pair_lists(P_SIZE)
    npair = len(first)
    blocks = lower_panel.reshape(group, P_SIZE, B, W)
    gram = jnp.einsum("siac,sjbc->sijab", blocks, blocks, precision=lax.Precision.HIGHEST)
    gram = gram.reshape(group, P_SIZE * P_SIZE, B, B)
    contribution = gram[:, first * P_SIZE + second]

    quarters = lax.all_to_all(contribution, "narrow", split_axis=2, concat_axis=0, tiled=True)
    quarter_rows = quarters.shape[2]
    pair_rows = supers_here * npair
    quarters = quarters.reshape(pair_rows, quarter_rows, B)

    capacity = max(2, (pair_rows + wide_count - 1) // wide_count)
    owners = pair_owner[:, 0]
    owner_table = (owners[:, None] == jnp.arange(wide_count, dtype=jnp.int32)[None, :]).astype(
        jnp.int32
    )
    earlier = jnp.cumsum(owner_table, axis=0) - owner_table
    rank_here = jnp.sum(earlier * owner_table, axis=1)
    position = owners * capacity + rank_here
    buffer_rows = wide_count * capacity
    row_slots = T_DEV * narrow_count
    slot_ids = jnp.full((buffer_rows,), -1.0, jnp.float32).at[position].set(
        pair_slot.astype(jnp.float32)
    )
    source_row = jnp.zeros((buffer_rows,), jnp.int32).at[position].set(
        jnp.arange(pair_rows, dtype=jnp.int32)
    )
    filled = jnp.zeros((buffer_rows,), jnp.bool_).at[position].set(True)
    send_buffer = jnp.where(filled[:, None, None], quarters[source_row], 0.0)
    meta = jnp.zeros((wide_count, 8, B), jnp.float32)
    meta = meta.at[:, 0, :capacity].set(slot_ids.reshape(wide_count, capacity))
    send_buffer = jnp.concatenate(
        [send_buffer.reshape(wide_count, capacity * quarter_rows, B), meta], axis=1
    )
    send_buffer, factor, lower_panel = lax.optimization_barrier((send_buffer, factor, lower_panel))
    received = lax.all_to_all(send_buffer, "wide", split_axis=0, concat_axis=0, tiled=True)
    factor_back = columns_out(factor, narrow_count, col_width, 0)
    lower_back = columns_out(lower_panel, narrow_count, col_width, 1)
    received, factor_back, lower_back = lax.optimization_barrier((received, factor_back, lower_back))
    got_slots = received[:, capacity * quarter_rows, :capacity].reshape(buffer_rows)
    got_slots = got_slots.astype(jnp.int32)
    received = received[:, : capacity * quarter_rows, :].reshape(buffer_rows, quarter_rows, B)
    slot_table = (got_slots[:, None] == jnp.arange(row_slots, dtype=jnp.int32)[None, :]).astype(
        jnp.float32
    )
    slot_sums = jnp.einsum("ri,rab->iab", slot_table, received, precision=lax.Precision.HIGHEST)
    slot_sums = slot_sums.reshape(narrow_count, T_DEV, quarter_rows, B)
    summed = lax.all_to_all(slot_sums, "narrow", split_axis=0, concat_axis=2, tiled=True)
    summed = summed.reshape(T_DEV, B, B)
    return (factor_back, lower_back, ancestor - summed)


def solution(mesh):
    placed = (
        P("wide", None, "narrow"),
        P("wide", None, "narrow"),
        P("wide"),
        P("wide", None),
        P("wide"),
        P(("wide", "narrow"), None, None),
    )
    return jax.shard_map(
        local,
        mesh=mesh,
        in_specs=placed,
        out_specs=(
            P("wide", None, "narrow"),
            P("wide", None, "narrow"),
            P(("wide", "narrow"), None, None),
        ),
        check_vma=False,
    )
```

```python
import functools

import jax
import jax.numpy as jnp
import numpy as np
from jax import lax
from jax.experimental import pallas as pl
from jax.experimental.pallas import tpu as pltpu
from jax.sharding import PartitionSpec as P

MESH = pl.DeviceIdType.MESH

W = 512
B = 128
P_SIZE = 8
T_DEV = 2


def pair_lists(count):
    first = []
    second = []
    for outer in range(count):
        for inner in range(outer + 1):
            first.append(outer)
            second.append(inner)
    return (np.array(first, np.int32), np.array(second, np.int32))


def columns_out_kernel(x_ref, y_ref, send_sem, recv_sem, own_sem, *, count, group, width):
    me = lax.axis_index("narrow")
    wide = lax.axis_index("wide")
    barrier = pltpu.get_barrier_semaphore()
    for d in range(1, count):
        peer = lax.rem(me + d, count)
        pl.semaphore_signal(barrier, inc=1, device_id=(wide, peer), device_id_type=MESH)
    pl.semaphore_wait(barrier, count - 1)
    mine = y_ref.at[pl.ds(me * group, group)]
    own = pltpu.make_async_copy(
        x_ref.at[:, :, pl.ds(pl.multiple_of(me * width, width), width)], mine, own_sem
    )
    own.start()
    copies = []
    for d in range(1, count):
        peer = lax.rem(me + d, count)
        copy = pltpu.make_async_remote_copy(
            src_ref=x_ref.at[:, :, pl.ds(pl.multiple_of(peer * width, width), width)],
            dst_ref=mine,
            send_sem=send_sem.at[d - 1],
            recv_sem=recv_sem.at[d - 1],
            device_id=(wide, peer),
            device_id_type=MESH,
        )
        copy.start()
        copies.append(copy)
    own.wait()
    for copy in copies:
        copy.wait()


def columns_out(x, count, width, collective_id):
    group, rows, _ = x.shape
    nbytes = x.size * 4
    return pl.pallas_call(
        functools.partial(columns_out_kernel, count=count, group=group, width=width),
        out_shape=jax.ShapeDtypeStruct((group * count, rows, width), x.dtype),
        in_specs=[pl.BlockSpec(memory_space=pl.ANY)],
        out_specs=pl.BlockSpec(memory_space=pl.ANY),
        scratch_shapes=[
            pltpu.SemaphoreType.DMA((count - 1,)),
            pltpu.SemaphoreType.DMA((count - 1,)),
            pltpu.SemaphoreType.DMA,
        ],
        compiler_params=pltpu.CompilerParams(collective_id=collective_id, has_side_effects=True),
        cost_estimate=pl.CostEstimate(flops=0, bytes_accessed=2 * nbytes, transcendentals=0),
    )(x)


def block_chol_kernel(a_ref, l_ref, inv_ref, work, upper, elim):
    n = a_ref.shape[0]
    phase = 32
    work[...] = a_ref[...]
    rows = lax.broadcasted_iota(jnp.int32, (n, n), 0)
    cols = lax.broadcasted_iota(jnp.int32, (n, n), 1)
    elim[...] = (rows == cols).astype(jnp.float32)
    lane = lax.broadcasted_iota(jnp.int32, (1, n), 1)

    for top in range(0, n, phase):
        height = n - top
        tail_cols = lax.broadcasted_iota(jnp.int32, (height, n), 1)
        tail_rows = top + lax.broadcasted_iota(jnp.int32, (height, 1), 0)

        def step(j, carry, top=top, height=height, tail_cols=tail_cols, tail_rows=tail_rows):
            r = work[pl.ds(j, 1), :]
            piv = jnp.sum(jnp.where(lane == j, r, 0.0), axis=1, keepdims=True)
            root = jnp.sqrt(piv)
            scale = 1.0 / root
            u_row = jnp.where(lane >= j, r * scale, 0.0)
            upper[pl.ds(j, 1), :] = u_row
            e_row = elim[pl.ds(j, 1), :]
            inv_ref[pl.ds(j, 1), :] = e_row * scale
            whole = work[top:, :]
            u_col = jnp.sum(jnp.where(tail_cols == j, whole, 0.0), axis=1, keepdims=True) * scale
            u_col = jnp.where(tail_rows >= j, u_col, 0.0)
            work[top:, :] = whole - u_col * u_row
            mult = jnp.where(tail_rows > j, u_col * scale, 0.0)
            elim[top:, :] = elim[top:, :] - mult * e_row
            return carry

        lax.fori_loop(top, top + phase, step, 0)
    l_ref[...] = jnp.transpose(upper[...])


def block_chol(a):
    n = a.shape[-1]
    return pl.pallas_call(
        block_chol_kernel,
        out_shape=(jax.ShapeDtypeStruct((n, n), jnp.float32), jax.ShapeDtypeStruct((n, n), jnp.float32)),
        in_specs=[pl.BlockSpec(memory_space=pltpu.VMEM)],
        out_specs=(pl.BlockSpec(memory_space=pltpu.VMEM), pl.BlockSpec(memory_space=pltpu.VMEM)),
        scratch_shapes=[pltpu.VMEM((n, n), jnp.float32)] * 3,
    )(a)


def mm(a, b):
    return jnp.einsum("sik,skj->sij", a, b, precision=lax.Precision.HIGHEST)


def mm_t(a, b):
    return jnp.einsum("sik,sjk->sij", a, b, precision=lax.Precision.HIGHEST)


def blocked_cholesky(matrix):
    batch, size, _ = matrix.shape
    nblk = size // B
    eye = jnp.broadcast_to(jnp.eye(B, dtype=jnp.float32), (batch, B, B))
    trailing = matrix
    diag_l, diag_inv, below = [], [], []
    inverse_rows = []
    for k in range(nblk):
        head = trailing[:, :B, :B]
        pieces = [block_chol(head[b]) for b in range(batch)]
        l_kk = jnp.stack([p[0] for p in pieces])
        i_kk = jnp.stack([p[1] for p in pieces])
        diag_l.append(l_kk)
        diag_inv.append(i_kk)
        if k > 0:
            left = jnp.concatenate([below[j][:, (k - j - 1) * B:(k - j) * B, :] for j in range(k)], axis=2)
            upper = jnp.concatenate(inverse_rows, axis=1)
            rest = -mm(left, upper)
            rest = jnp.concatenate([rest[:, :, :k * B], eye, rest[:, :, (k + 1) * B:]], axis=2)
            inverse_rows.append(mm(i_kk, rest))
        else:
            inverse_rows.append(jnp.concatenate(
                [i_kk, jnp.zeros((batch, B, size - B), jnp.float32)], axis=2))
        if k < nblk - 1:
            panel_k = mm_t(trailing[:, B:, :B], i_kk)
            below.append(panel_k)
            trailing = trailing[:, B:, B:] - mm_t(panel_k, panel_k)
    columns = []
    for k in range(nblk):
        parts = []
        if k > 0:
            parts.append(jnp.zeros((batch, k * B, B), jnp.float32))
        parts.append(diag_l[k])
        if k < nblk - 1:
            parts.append(below[k])
        columns.append(jnp.concatenate(parts, axis=1))
    factor = jnp.concatenate(columns, axis=2)
    inverse = jnp.concatenate(inverse_rows, axis=1)
    return factor, inverse


def local(diag_block, panel, panel_count, pair_owner, pair_slot, ancestor):
    supers_here = diag_block.shape[0]
    col_width = diag_block.shape[2]
    diag_rows = diag_block.shape[1]
    narrow_index = lax.axis_index("narrow")
    narrow_count = lax.axis_size("narrow")
    wide_count = lax.axis_size("wide")
    group = supers_here // narrow_count

    whole_diag = lax.all_to_all(diag_block, "narrow", split_axis=0, concat_axis=2, tiled=True)
    whole_panel = lax.all_to_all(panel, "narrow", split_axis=0, concat_axis=2, tiled=True)

    factor, inverse = blocked_cholesky(whole_diag)
    lower_panel = jnp.einsum(
        "srk,sck->src", whole_panel, inverse, precision=lax.Precision.HIGHEST
    )
    counts = lax.dynamic_slice_in_dim(panel_count, narrow_index * group, group)
    block_index = jnp.arange(P_SIZE * B, dtype=jnp.int32) // B
    live = (block_index[None, :] < counts[:, None]).astype(jnp.float32)
    lower_panel = lower_panel * live[:, :, None]

    first, second = pair_lists(P_SIZE)
    npair = len(first)
    blocks = lower_panel.reshape(group, P_SIZE, B, W)
    gram = jnp.einsum("siac,sjbc->sijab", blocks, blocks, precision=lax.Precision.HIGHEST)
    gram = gram.reshape(group, P_SIZE * P_SIZE, B, B)
    contribution = gram[:, first * P_SIZE + second]

    quarters = lax.all_to_all(contribution, "narrow", split_axis=2, concat_axis=0, tiled=True)
    quarter_rows = quarters.shape[2]
    pair_rows = supers_here * npair
    quarters = quarters.reshape(pair_rows, quarter_rows, B)

    capacity = max(2, (pair_rows + wide_count - 1) // wide_count)
    owners = pair_owner[:, 0]
    owner_table = (owners[:, None] == jnp.arange(wide_count, dtype=jnp.int32)[None, :]).astype(
        jnp.int32
    )
    earlier = jnp.cumsum(owner_table, axis=0) - owner_table
    rank_here = jnp.sum(earlier * owner_table, axis=1)
    position = owners * capacity + rank_here
    buffer_rows = wide_count * capacity
    row_slots = T_DEV * narrow_count
    slot_ids = jnp.full((buffer_rows,), -1.0, jnp.float32).at[position].set(
        pair_slot.astype(jnp.float32)
    )
    source_row = jnp.zeros((buffer_rows,), jnp.int32).at[position].set(
        jnp.arange(pair_rows, dtype=jnp.int32)
    )
    filled = jnp.zeros((buffer_rows,), jnp.bool_).at[position].set(True)
    send_buffer = jnp.where(filled[:, None, None], quarters[source_row], 0.0)
    meta = jnp.zeros((wide_count, 8, B), jnp.float32)
    meta = meta.at[:, 0, :capacity].set(slot_ids.reshape(wide_count, capacity))
    send_buffer = jnp.concatenate(
        [send_buffer.reshape(wide_count, capacity * quarter_rows, B), meta], axis=1
    )
    send_buffer, factor, lower_panel = lax.optimization_barrier((send_buffer, factor, lower_panel))
    received = lax.all_to_all(send_buffer, "wide", split_axis=0, concat_axis=0, tiled=True)
    factor_back = columns_out(factor, narrow_count, col_width, 0)
    lower_back = columns_out(lower_panel, narrow_count, col_width, 1)
    received, factor_back, lower_back = lax.optimization_barrier((received, factor_back, lower_back))
    got_slots = received[:, capacity * quarter_rows, :capacity].reshape(buffer_rows)
    got_slots = got_slots.astype(jnp.int32)
    received = received[:, : capacity * quarter_rows, :].reshape(buffer_rows, quarter_rows, B)
    slot_table = (got_slots[:, None] == jnp.arange(row_slots, dtype=jnp.int32)[None, :]).astype(
        jnp.float32
    )
    slot_sums = jnp.einsum("ri,rab->iab", slot_table, received, precision=lax.Precision.HIGHEST)
    slot_sums = slot_sums.reshape(narrow_count, T_DEV, quarter_rows, B)
    summed = lax.all_to_all(slot_sums, "narrow", split_axis=0, concat_axis=2, tiled=True)
    summed = summed.reshape(T_DEV, B, B)
    return (factor_back, lower_back, ancestor - summed)


def solution(mesh):
    placed = (
        P("wide", None, "narrow"),
        P("wide", None, "narrow"),
        P("wide"),
        P("wide", None),
        P("wide"),
        P(("wide", "narrow"), None, None),
    )
    return jax.shard_map(
        local,
        mesh=mesh,
        in_specs=placed,
        out_specs=(
            P("wide", None, "narrow"),
            P("wide", None, "narrow"),
            P(("wide", "narrow"), None, None),
        ),
        check_vma=False,
    )
```

```python
import functools

import jax
import jax.numpy as jnp
import numpy as np
from jax import lax
from jax.experimental import pallas as pl
from jax.experimental.pallas import tpu as pltpu
from jax.sharding import PartitionSpec as P

MESH = pl.DeviceIdType.MESH

W = 512
B = 128
P_SIZE = 8
T_DEV = 2


def pair_lists(count):
    first = []
    second = []
    for outer in range(count):
        for inner in range(outer + 1):
            first.append(outer)
            second.append(inner)
    return (np.array(first, np.int32), np.array(second, np.int32))


def columns_out_kernel(x_ref, y_ref, send_sem, recv_sem, own_sem, *, count, group, width):
    me = lax.axis_index("narrow")
    wide = lax.axis_index("wide")
    barrier = pltpu.get_barrier_semaphore()
    for d in range(1, count):
        peer = lax.rem(me + d, count)
        pl.semaphore_signal(barrier, inc=1, device_id=(wide, peer), device_id_type=MESH)
    pl.semaphore_wait(barrier, count - 1)
    mine = y_ref.at[pl.ds(me * group, group)]
    own = pltpu.make_async_copy(
        x_ref.at[:, :, pl.ds(pl.multiple_of(me * width, width), width)], mine, own_sem
    )
    own.start()
    copies = []
    for d in range(1, count):
        peer = lax.rem(me + d, count)
        copy = pltpu.make_async_remote_copy(
            src_ref=x_ref.at[:, :, pl.ds(pl.multiple_of(peer * width, width), width)],
            dst_ref=mine,
            send_sem=send_sem.at[d - 1],
            recv_sem=recv_sem.at[d - 1],
            device_id=(wide, peer),
            device_id_type=MESH,
        )
        copy.start()
        copies.append(copy)
    own.wait()
    for copy in copies:
        copy.wait()


def columns_out(x, count, width, collective_id):
    group, rows, _ = x.shape
    nbytes = x.size * 4
    return pl.pallas_call(
        functools.partial(columns_out_kernel, count=count, group=group, width=width),
        out_shape=jax.ShapeDtypeStruct((group * count, rows, width), x.dtype),
        in_specs=[pl.BlockSpec(memory_space=pl.ANY)],
        out_specs=pl.BlockSpec(memory_space=pl.ANY),
        scratch_shapes=[
            pltpu.SemaphoreType.DMA((count - 1,)),
            pltpu.SemaphoreType.DMA((count - 1,)),
            pltpu.SemaphoreType.DMA,
        ],
        compiler_params=pltpu.CompilerParams(collective_id=collective_id, has_side_effects=True),
        cost_estimate=pl.CostEstimate(flops=0, bytes_accessed=2 * nbytes, transcendentals=0),
    )(x)


def block_chol_kernel(a_ref, l_ref, inv_ref, work, upper, elim):
    n = a_ref.shape[0]
    phase = 32
    work[...] = a_ref[...]
    rows = lax.broadcasted_iota(jnp.int32, (n, n), 0)
    cols = lax.broadcasted_iota(jnp.int32, (n, n), 1)
    elim[...] = (rows == cols).astype(jnp.float32)
    lane = lax.broadcasted_iota(jnp.int32, (1, n), 1)

    for top in range(0, n, phase):
        height = n - top
        tail_cols = lax.broadcasted_iota(jnp.int32, (height, n), 1)
        tail_rows = top + lax.broadcasted_iota(jnp.int32, (height, 1), 0)

        def step(j, carry, top=top, height=height, tail_cols=tail_cols, tail_rows=tail_rows):
            r = work[pl.ds(j, 1), :]
            piv = jnp.sum(jnp.where(lane == j, r, 0.0), axis=1, keepdims=True)
            root = jnp.sqrt(piv)
            scale = 1.0 / root
            u_row = jnp.where(lane >= j, r * scale, 0.0)
            upper[pl.ds(j, 1), :] = u_row
            e_row = elim[pl.ds(j, 1), :]
            inv_ref[pl.ds(j, 1), :] = e_row * scale
            whole = work[top:, :]
            u_col = jnp.sum(jnp.where(tail_cols == j, whole, 0.0), axis=1, keepdims=True) * scale
            u_col = jnp.where(tail_rows >= j, u_col, 0.0)
            work[top:, :] = whole - u_col * u_row
            mult = jnp.where(tail_rows > j, u_col * scale, 0.0)
            elim[top:, :] = elim[top:, :] - mult * e_row
            return carry

        lax.fori_loop(top, top + phase, step, 0)
    l_ref[...] = jnp.transpose(upper[...])


def block_chol(a):
    n = a.shape[-1]
    return pl.pallas_call(
        block_chol_kernel,
        out_shape=(jax.ShapeDtypeStruct((n, n), jnp.float32), jax.ShapeDtypeStruct((n, n), jnp.float32)),
        in_specs=[pl.BlockSpec(memory_space=pltpu.VMEM)],
        out_specs=(pl.BlockSpec(memory_space=pltpu.VMEM), pl.BlockSpec(memory_space=pltpu.VMEM)),
        scratch_shapes=[pltpu.VMEM((n, n), jnp.float32)] * 3,
    )(a)


def mm(a, b):
    return jnp.einsum("sik,skj->sij", a, b, precision=lax.Precision.HIGHEST)


def mm_t(a, b):
    return jnp.einsum("sik,sjk->sij", a, b, precision=lax.Precision.HIGHEST)


def blocked_cholesky(matrix):
    batch, size, _ = matrix.shape
    nblk = size // B
    eye = jnp.broadcast_to(jnp.eye(B, dtype=jnp.float32), (batch, B, B))
    trailing = matrix
    diag_l, diag_inv, below = [], [], []
    inverse_rows = []
    for k in range(nblk):
        head = trailing[:, :B, :B]
        pieces = [block_chol(head[b]) for b in range(batch)]
        l_kk = jnp.stack([p[0] for p in pieces])
        i_kk = jnp.stack([p[1] for p in pieces])
        diag_l.append(l_kk)
        diag_inv.append(i_kk)
        if k > 0:
            left = jnp.concatenate([below[j][:, (k - j - 1) * B:(k - j) * B, :] for j in range(k)], axis=2)
            upper = jnp.concatenate(inverse_rows, axis=1)
            rest = -mm(left, upper)
            rest = jnp.concatenate([rest[:, :, :k * B], eye, rest[:, :, (k + 1) * B:]], axis=2)
            inverse_rows.append(mm(i_kk, rest))
        else:
            inverse_rows.append(jnp.concatenate(
                [i_kk, jnp.zeros((batch, B, size - B), jnp.float32)], axis=2))
        if k < nblk - 1:
            panel_k = mm_t(trailing[:, B:, :B], i_kk)
            below.append(panel_k)
            trailing = trailing[:, B:, B:] - mm_t(panel_k, panel_k)
    columns = []
    for k in range(nblk):
        parts = []
        if k > 0:
            parts.append(jnp.zeros((batch, k * B, B), jnp.float32))
        parts.append(diag_l[k])
        if k < nblk - 1:
            parts.append(below[k])
        columns.append(jnp.concatenate(parts, axis=1))
    factor = jnp.concatenate(columns, axis=2)
    inverse = jnp.concatenate(inverse_rows, axis=1)
    return factor, inverse


def local(diag_block, panel, panel_count, pair_owner, pair_slot, ancestor):
    supers_here = diag_block.shape[0]
    col_width = diag_block.shape[2]
    diag_rows = diag_block.shape[1]
    narrow_index = lax.axis_index("narrow")
    narrow_count = lax.axis_size("narrow")
    wide_count = lax.axis_size("wide")
    group = supers_here // narrow_count

    whole_diag = lax.all_to_all(diag_block, "narrow", split_axis=0, concat_axis=2, tiled=True)
    whole_panel = lax.all_to_all(panel, "narrow", split_axis=0, concat_axis=2, tiled=True)

    factor, inverse = blocked_cholesky(whole_diag)
    lower_panel = jnp.einsum(
        "srk,sck->src", whole_panel, inverse, precision=lax.Precision.HIGHEST
    )
    counts = lax.dynamic_slice_in_dim(panel_count, narrow_index * group, group)
    block_index = jnp.arange(P_SIZE * B, dtype=jnp.int32) // B
    live = (block_index[None, :] < counts[:, None]).astype(jnp.float32)
    lower_panel = lower_panel * live[:, :, None]

    first, second = pair_lists(P_SIZE)
    npair = len(first)
    blocks = lower_panel.reshape(group, P_SIZE, B, W)
    split = int(np.searchsorted(first, 5))
    pieces = []
    for lo, hi in ((0, split), (split, npair)):
        part = jnp.einsum(
            "spac,spbc->spab",
            blocks[:, first[lo:hi]],
            blocks[:, second[lo:hi]],
            precision=lax.Precision.HIGHEST,
        )
        pieces.append(lax.all_to_all(part, "narrow", split_axis=2, concat_axis=0, tiled=True))
    quarters = jnp.concatenate(pieces, axis=1)
    quarter_rows = quarters.shape[2]
    pair_rows = supers_here * npair
    quarters = quarters.reshape(pair_rows, quarter_rows, B)

    capacity = max(2, (pair_rows + wide_count - 1) // wide_count)
    owners = pair_owner[:, 0]
    owner_table = (owners[:, None] == jnp.arange(wide_count, dtype=jnp.int32)[None, :]).astype(
        jnp.int32
    )
    earlier = jnp.cumsum(owner_table, axis=0) - owner_table
    rank_here = jnp.sum(earlier * owner_table, axis=1)
    position = owners * capacity + rank_here
    buffer_rows = wide_count * capacity
    row_slots = T_DEV * narrow_count
    slot_ids = jnp.full((buffer_rows,), -1.0, jnp.float32).at[position].set(
        pair_slot.astype(jnp.float32)
    )
    source_row = jnp.zeros((buffer_rows,), jnp.int32).at[position].set(
        jnp.arange(pair_rows, dtype=jnp.int32)
    )
    filled = jnp.zeros((buffer_rows,), jnp.bool_).at[position].set(True)
    send_buffer = jnp.where(filled[:, None, None], quarters[source_row], 0.0)
    meta = jnp.zeros((wide_count, 8, B), jnp.float32)
    meta = meta.at[:, 0, :capacity].set(slot_ids.reshape(wide_count, capacity))
    send_buffer = jnp.concatenate(
        [send_buffer.reshape(wide_count, capacity * quarter_rows, B), meta], axis=1
    )
    send_buffer, factor, lower_panel = lax.optimization_barrier((send_buffer, factor, lower_panel))
    received = lax.all_to_all(send_buffer, "wide", split_axis=0, concat_axis=0, tiled=True)
    factor_back = columns_out(factor, narrow_count, col_width, 0)
    lower_back = columns_out(lower_panel, narrow_count, col_width, 1)
    received, factor_back, lower_back = lax.optimization_barrier((received, factor_back, lower_back))
    got_slots = received[:, capacity * quarter_rows, :capacity].reshape(buffer_rows)
    got_slots = got_slots.astype(jnp.int32)
    received = received[:, : capacity * quarter_rows, :].reshape(buffer_rows, quarter_rows, B)
    slot_table = (got_slots[:, None] == jnp.arange(row_slots, dtype=jnp.int32)[None, :]).astype(
        jnp.float32
    )
    slot_sums = jnp.einsum("ri,rab->iab", slot_table, received, precision=lax.Precision.HIGHEST)
    slot_sums = slot_sums.reshape(narrow_count, T_DEV, quarter_rows, B)
    summed = lax.all_to_all(slot_sums, "narrow", split_axis=0, concat_axis=2, tiled=True)
    summed = summed.reshape(T_DEV, B, B)
    return (factor_back, lower_back, ancestor - summed)


def solution(mesh):
    placed = (
        P("wide", None, "narrow"),
        P("wide", None, "narrow"),
        P("wide"),
        P("wide", None),
        P("wide"),
        P(("wide", "narrow"), None, None),
    )
    return jax.shard_map(
        local,
        mesh=mesh,
        in_specs=placed,
        out_specs=(
            P("wide", None, "narrow"),
            P("wide", None, "narrow"),
            P(("wide", "narrow"), None, None),
        ),
        check_vma=False,
    )
```

```python
import functools

import jax
import jax.numpy as jnp
import numpy as np
from jax import lax
from jax.experimental import pallas as pl
from jax.experimental.pallas import tpu as pltpu
from jax.sharding import PartitionSpec as P

MESH = pl.DeviceIdType.MESH

W = 512
B = 128
P_SIZE = 8
T_DEV = 2


def pair_lists(count):
    first = []
    second = []
    for outer in range(count):
        for inner in range(outer + 1):
            first.append(outer)
            second.append(inner)
    return (np.array(first, np.int32), np.array(second, np.int32))


def columns_out_kernel(x_ref, y_ref, send_sem, recv_sem, own_sem, *, count, group, width):
    me = lax.axis_index("narrow")
    wide = lax.axis_index("wide")
    barrier = pltpu.get_barrier_semaphore()
    for d in range(1, count):
        peer = lax.rem(me + d, count)
        pl.semaphore_signal(barrier, inc=1, device_id=(wide, peer), device_id_type=MESH)
    pl.semaphore_wait(barrier, count - 1)
    mine = y_ref.at[pl.ds(me * group, group)]
    own = pltpu.make_async_copy(
        x_ref.at[:, :, pl.ds(pl.multiple_of(me * width, width), width)], mine, own_sem
    )
    own.start()
    copies = []
    for d in range(1, count):
        peer = lax.rem(me + d, count)
        copy = pltpu.make_async_remote_copy(
            src_ref=x_ref.at[:, :, pl.ds(pl.multiple_of(peer * width, width), width)],
            dst_ref=mine,
            send_sem=send_sem.at[d - 1],
            recv_sem=recv_sem.at[d - 1],
            device_id=(wide, peer),
            device_id_type=MESH,
        )
        copy.start()
        copies.append(copy)
    own.wait()
    for copy in copies:
        copy.wait()


def columns_out(x, count, width, collective_id):
    group, rows, _ = x.shape
    nbytes = x.size * 4
    return pl.pallas_call(
        functools.partial(columns_out_kernel, count=count, group=group, width=width),
        out_shape=jax.ShapeDtypeStruct((group * count, rows, width), x.dtype),
        in_specs=[pl.BlockSpec(memory_space=pl.ANY)],
        out_specs=pl.BlockSpec(memory_space=pl.ANY),
        scratch_shapes=[
            pltpu.SemaphoreType.DMA((count - 1,)),
            pltpu.SemaphoreType.DMA((count - 1,)),
            pltpu.SemaphoreType.DMA,
        ],
        compiler_params=pltpu.CompilerParams(collective_id=collective_id, has_side_effects=True),
        cost_estimate=pl.CostEstimate(flops=0, bytes_accessed=2 * nbytes, transcendentals=0),
    )(x)


def block_chol_kernel(a_ref, l_ref, inv_ref, work, upper, elim):
    n = a_ref.shape[0]
    phase = 32
    work[...] = a_ref[...]
    rows = lax.broadcasted_iota(jnp.int32, (n, n), 0)
    cols = lax.broadcasted_iota(jnp.int32, (n, n), 1)
    elim[...] = (rows == cols).astype(jnp.float32)
    lane = lax.broadcasted_iota(jnp.int32, (1, n), 1)

    for top in range(0, n, phase):
        height = n - top
        tail_cols = lax.broadcasted_iota(jnp.int32, (height, n), 1)
        tail_rows = top + lax.broadcasted_iota(jnp.int32, (height, 1), 0)

        def step(j, carry, top=top, tail_cols=tail_cols, tail_rows=tail_rows):
            r = work[pl.ds(j, 1), :]
            whole = work[top:, :]
            col = jnp.sum(jnp.where(tail_cols == j, whole, 0.0), axis=1, keepdims=True)
            piv = jnp.sum(jnp.where(lane == j, r, 0.0), axis=1, keepdims=True)
            inv_piv = 1.0 / piv
            r_live = jnp.where(lane >= j, r, 0.0)
            mult = jnp.where(tail_rows > j, col * inv_piv, 0.0)
            work[top:, :] = whole - mult * r_live
            e_row = elim[pl.ds(j, 1), :]
            elim[top:, :] = elim[top:, :] - mult * e_row
            scale = 1.0 / jnp.sqrt(piv)
            upper[pl.ds(j, 1), :] = r_live * scale
            inv_ref[pl.ds(j, 1), :] = e_row * scale
            return carry

        lax.fori_loop(top, top + phase, step, 0)
    l_ref[...] = jnp.transpose(upper[...])


def block_chol(a):
    n = a.shape[-1]
    return pl.pallas_call(
        block_chol_kernel,
        out_shape=(jax.ShapeDtypeStruct((n, n), jnp.float32), jax.ShapeDtypeStruct((n, n), jnp.float32)),
        in_specs=[pl.BlockSpec(memory_space=pltpu.VMEM)],
        out_specs=(pl.BlockSpec(memory_space=pltpu.VMEM), pl.BlockSpec(memory_space=pltpu.VMEM)),
        scratch_shapes=[pltpu.VMEM((n, n), jnp.float32)] * 3,
    )(a)


def mm(a, b):
    return jnp.einsum("sik,skj->sij", a, b, precision=lax.Precision.HIGHEST)


def mm_t(a, b):
    return jnp.einsum("sik,sjk->sij", a, b, precision=lax.Precision.HIGHEST)


def blocked_cholesky(matrix):
    batch, size, _ = matrix.shape
    nblk = size // B
    eye = jnp.broadcast_to(jnp.eye(B, dtype=jnp.float32), (batch, B, B))
    trailing = matrix
    diag_l, diag_inv, below = [], [], []
    inverse_rows = []
    for k in range(nblk):
        head = trailing[:, :B, :B]
        pieces = [block_chol(head[b]) for b in range(batch)]
        l_kk = jnp.stack([p[0] for p in pieces])
        i_kk = jnp.stack([p[1] for p in pieces])
        diag_l.append(l_kk)
        diag_inv.append(i_kk)
        if k > 0:
            left = jnp.concatenate([below[j][:, (k - j - 1) * B:(k - j) * B, :] for j in range(k)], axis=2)
            upper = jnp.concatenate(inverse_rows, axis=1)
            rest = -mm(left, upper)
            rest = jnp.concatenate([rest[:, :, :k * B], eye, rest[:, :, (k + 1) * B:]], axis=2)
            inverse_rows.append(mm(i_kk, rest))
        else:
            inverse_rows.append(jnp.concatenate(
                [i_kk, jnp.zeros((batch, B, size - B), jnp.float32)], axis=2))
        if k < nblk - 1:
            panel_k = mm_t(trailing[:, B:, :B], i_kk)
            below.append(panel_k)
            trailing = trailing[:, B:, B:] - mm_t(panel_k, panel_k)
    columns = []
    for k in range(nblk):
        parts = []
        if k > 0:
            parts.append(jnp.zeros((batch, k * B, B), jnp.float32))
        parts.append(diag_l[k])
        if k < nblk - 1:
            parts.append(below[k])
        columns.append(jnp.concatenate(parts, axis=1))
    factor = jnp.concatenate(columns, axis=2)
    inverse = jnp.concatenate(inverse_rows, axis=1)
    return factor, inverse


def local(diag_block, panel, panel_count, pair_owner, pair_slot, ancestor):
    supers_here = diag_block.shape[0]
    col_width = diag_block.shape[2]
    diag_rows = diag_block.shape[1]
    narrow_index = lax.axis_index("narrow")
    narrow_count = lax.axis_size("narrow")
    wide_count = lax.axis_size("wide")
    group = supers_here // narrow_count

    whole_diag = lax.all_to_all(diag_block, "narrow", split_axis=0, concat_axis=2, tiled=True)
    whole_panel = lax.all_to_all(panel, "narrow", split_axis=0, concat_axis=2, tiled=True)

    factor, inverse = blocked_cholesky(whole_diag)
    lower_panel = jnp.einsum(
        "srk,sck->src", whole_panel, inverse, precision=lax.Precision.HIGHEST
    )
    counts = lax.dynamic_slice_in_dim(panel_count, narrow_index * group, group)
    block_index = jnp.arange(P_SIZE * B, dtype=jnp.int32) // B
    live = (block_index[None, :] < counts[:, None]).astype(jnp.float32)
    lower_panel = lower_panel * live[:, :, None]

    first, second = pair_lists(P_SIZE)
    npair = len(first)
    blocks = lower_panel.reshape(group, P_SIZE, B, W)
    gram = jnp.einsum("siac,sjbc->sijab", blocks, blocks, precision=lax.Precision.HIGHEST)
    gram = gram.reshape(group, P_SIZE * P_SIZE, B, B)
    contribution = gram[:, first * P_SIZE + second]

    quarters = lax.all_to_all(contribution, "narrow", split_axis=2, concat_axis=0, tiled=True)
    quarter_rows = quarters.shape[2]
    pair_rows = supers_here * npair
    quarters = quarters.reshape(pair_rows, quarter_rows, B)

    capacity = max(2, (pair_rows + wide_count - 1) // wide_count)
    owners = pair_owner[:, 0]
    owner_table = (owners[:, None] == jnp.arange(wide_count, dtype=jnp.int32)[None, :]).astype(
        jnp.int32
    )
    earlier = jnp.cumsum(owner_table, axis=0) - owner_table
    rank_here = jnp.sum(earlier * owner_table, axis=1)
    position = owners * capacity + rank_here
    buffer_rows = wide_count * capacity
    row_slots = T_DEV * narrow_count
    slot_ids = jnp.full((buffer_rows,), -1.0, jnp.float32).at[position].set(
        pair_slot.astype(jnp.float32)
    )
    source_row = jnp.zeros((buffer_rows,), jnp.int32).at[position].set(
        jnp.arange(pair_rows, dtype=jnp.int32)
    )
    filled = jnp.zeros((buffer_rows,), jnp.bool_).at[position].set(True)
    send_buffer = jnp.where(filled[:, None, None], quarters[source_row], 0.0)
    meta = jnp.zeros((wide_count, 8, B), jnp.float32)
    meta = meta.at[:, 0, :capacity].set(slot_ids.reshape(wide_count, capacity))
    send_buffer = jnp.concatenate(
        [send_buffer.reshape(wide_count, capacity * quarter_rows, B), meta], axis=1
    )
    send_buffer, factor, lower_panel = lax.optimization_barrier((send_buffer, factor, lower_panel))
    received = lax.all_to_all(send_buffer, "wide", split_axis=0, concat_axis=0, tiled=True)
    factor_back = columns_out(factor, narrow_count, col_width, 0)
    lower_back = columns_out(lower_panel, narrow_count, col_width, 1)
    received, factor_back, lower_back = lax.optimization_barrier((received, factor_back, lower_back))
    got_slots = received[:, capacity * quarter_rows, :capacity].reshape(buffer_rows)
    got_slots = got_slots.astype(jnp.int32)
    received = received[:, : capacity * quarter_rows, :].reshape(buffer_rows, quarter_rows, B)
    slot_table = (got_slots[:, None] == jnp.arange(row_slots, dtype=jnp.int32)[None, :]).astype(
        jnp.float32
    )
    slot_sums = jnp.einsum("ri,rab->iab", slot_table, received, precision=lax.Precision.HIGHEST)
    slot_sums = slot_sums.reshape(narrow_count, T_DEV, quarter_rows, B)
    summed = lax.all_to_all(slot_sums, "narrow", split_axis=0, concat_axis=2, tiled=True)
    summed = summed.reshape(T_DEV, B, B)
    return (factor_back, lower_back, ancestor - summed)


def solution(mesh):
    placed = (
        P("wide", None, "narrow"),
        P("wide", None, "narrow"),
        P("wide"),
        P("wide", None),
        P("wide"),
        P(("wide", "narrow"), None, None),
    )
    return jax.shard_map(
        local,
        mesh=mesh,
        in_specs=placed,
        out_specs=(
            P("wide", None, "narrow"),
            P("wide", None, "narrow"),
            P(("wide", "narrow"), None, None),
        ),
        check_vma=False,
    )
```

```python
import functools

import jax
import jax.numpy as jnp
import numpy as np
from jax import lax
from jax.experimental import pallas as pl
from jax.experimental.pallas import tpu as pltpu
from jax.sharding import PartitionSpec as P

MESH = pl.DeviceIdType.MESH

W = 512
B = 128
P_SIZE = 8
T_DEV = 2


def pair_lists(count):
    first = []
    second = []
    for outer in range(count):
        for inner in range(outer + 1):
            first.append(outer)
            second.append(inner)
    return (np.array(first, np.int32), np.array(second, np.int32))


def columns_out_kernel(x_ref, y_ref, send_sem, recv_sem, own_sem, *, count, group, width):
    me = lax.axis_index("narrow")
    wide = lax.axis_index("wide")
    barrier = pltpu.get_barrier_semaphore()
    for d in range(1, count):
        peer = lax.rem(me + d, count)
        pl.semaphore_signal(barrier, inc=1, device_id=(wide, peer), device_id_type=MESH)
    pl.semaphore_wait(barrier, count - 1)
    mine = y_ref.at[pl.ds(me * group, group)]
    own = pltpu.make_async_copy(
        x_ref.at[:, :, pl.ds(pl.multiple_of(me * width, width), width)], mine, own_sem
    )
    own.start()
    copies = []
    for d in range(1, count):
        peer = lax.rem(me + d, count)
        copy = pltpu.make_async_remote_copy(
            src_ref=x_ref.at[:, :, pl.ds(pl.multiple_of(peer * width, width), width)],
            dst_ref=mine,
            send_sem=send_sem.at[d - 1],
            recv_sem=recv_sem.at[d - 1],
            device_id=(wide, peer),
            device_id_type=MESH,
        )
        copy.start()
        copies.append(copy)
    own.wait()
    for copy in copies:
        copy.wait()


def columns_out(x, count, width, collective_id):
    group, rows, _ = x.shape
    nbytes = x.size * 4
    return pl.pallas_call(
        functools.partial(columns_out_kernel, count=count, group=group, width=width),
        out_shape=jax.ShapeDtypeStruct((group * count, rows, width), x.dtype),
        in_specs=[pl.BlockSpec(memory_space=pl.ANY)],
        out_specs=pl.BlockSpec(memory_space=pl.ANY),
        scratch_shapes=[
            pltpu.SemaphoreType.DMA((count - 1,)),
            pltpu.SemaphoreType.DMA((count - 1,)),
            pltpu.SemaphoreType.DMA,
        ],
        compiler_params=pltpu.CompilerParams(collective_id=collective_id, has_side_effects=True),
        cost_estimate=pl.CostEstimate(flops=0, bytes_accessed=2 * nbytes, transcendentals=0),
    )(x)


def block_chol_kernel(a_ref, l_ref, inv_ref, work, upper, elim):
    n = a_ref.shape[0]
    phase = 32
    work[...] = a_ref[...]
    rows = lax.broadcasted_iota(jnp.int32, (n, n), 0)
    cols = lax.broadcasted_iota(jnp.int32, (n, n), 1)
    elim[...] = (rows == cols).astype(jnp.float32)
    lane = lax.broadcasted_iota(jnp.int32, (1, n), 1)

    for top in range(0, n, phase):
        height = n - top
        tail_cols = lax.broadcasted_iota(jnp.int32, (height, n), 1)
        tail_rows = top + lax.broadcasted_iota(jnp.int32, (height, 1), 0)

        def step(j, carry, top=top, tail_cols=tail_cols, tail_rows=tail_rows):
            r = work[pl.ds(j, 1), :]
            whole = work[top:, :]
            col = jnp.sum(jnp.where(tail_cols == j, whole, 0.0), axis=1, keepdims=True)
            piv = jnp.sum(jnp.where(lane == j, r, 0.0), axis=1, keepdims=True)
            inv_piv = 1.0 / piv
            r_live = jnp.where(lane >= j, r, 0.0)
            mult = jnp.where(tail_rows > j, col * inv_piv, 0.0)
            work[top:, :] = whole - mult * r_live
            e_row = elim[pl.ds(j, 1), :]
            elim[top:, :] = elim[top:, :] - mult * e_row
            scale = 1.0 / jnp.sqrt(piv)
            upper[pl.ds(j, 1), :] = r_live * scale
            inv_ref[pl.ds(j, 1), :] = e_row * scale
            return carry

        lax.fori_loop(top, top + phase, step, 0)
    l_ref[...] = jnp.transpose(upper[...])


def block_chol(a):
    n = a.shape[-1]
    return pl.pallas_call(
        block_chol_kernel,
        out_shape=(jax.ShapeDtypeStruct((n, n), jnp.float32), jax.ShapeDtypeStruct((n, n), jnp.float32)),
        in_specs=[pl.BlockSpec(memory_space=pltpu.VMEM)],
        out_specs=(pl.BlockSpec(memory_space=pltpu.VMEM), pl.BlockSpec(memory_space=pltpu.VMEM)),
        scratch_shapes=[pltpu.VMEM((n, n), jnp.float32)] * 3,
    )(a)


def mm(a, b):
    return jnp.einsum("sik,skj->sij", a, b, precision=lax.Precision.HIGHEST)


def mm_t(a, b):
    return jnp.einsum("sik,sjk->sij", a, b, precision=lax.Precision.HIGHEST)


def blocked_cholesky(matrix):
    batch, size, _ = matrix.shape
    nblk = size // B
    trailing = matrix
    diag_l, diag_inv, below = [], [], []
    for k in range(nblk):
        head = trailing[:, :B, :B]
        pieces = [block_chol(head[b]) for b in range(batch)]
        l_kk = jnp.stack([p[0] for p in pieces])
        i_kk = jnp.stack([p[1] for p in pieces])
        diag_l.append(l_kk)
        diag_inv.append(i_kk)
        if k < nblk - 1:
            panel_k = mm_t(trailing[:, B:, :B], i_kk)
            below.append(panel_k)
            trailing = trailing[:, B:, B:] - mm_t(panel_k, panel_k)
    columns = []
    for k in range(nblk):
        parts = []
        if k > 0:
            parts.append(jnp.zeros((batch, k * B, B), jnp.float32))
        parts.append(diag_l[k])
        if k < nblk - 1:
            parts.append(below[k])
        columns.append(jnp.concatenate(parts, axis=1))
    factor = jnp.concatenate(columns, axis=2)
    return factor, diag_inv, below


def solve_panel(panel, diag_inv, below):
    done = []
    for k, i_kk in enumerate(diag_inv):
        rhs = panel[:, :, k * B:(k + 1) * B]
        if k > 0:
            left = jnp.concatenate(
                [below[j][:, (k - j - 1) * B:(k - j) * B, :] for j in range(k)], axis=2
            )
            rhs = rhs - mm_t(jnp.concatenate(done, axis=2), left)
        done.append(mm_t(rhs, i_kk))
    return jnp.concatenate(done, axis=2)


def local(diag_block, panel, panel_count, pair_owner, pair_slot, ancestor):
    supers_here = diag_block.shape[0]
    col_width = diag_block.shape[2]
    diag_rows = diag_block.shape[1]
    narrow_index = lax.axis_index("narrow")
    narrow_count = lax.axis_size("narrow")
    wide_count = lax.axis_size("wide")
    group = supers_here // narrow_count

    whole_diag = lax.all_to_all(diag_block, "narrow", split_axis=0, concat_axis=2, tiled=True)
    whole_panel = lax.all_to_all(panel, "narrow", split_axis=0, concat_axis=2, tiled=True)

    factor, diag_inv, below = blocked_cholesky(whole_diag)
    lower_panel = solve_panel(whole_panel, diag_inv, below)
    counts = lax.dynamic_slice_in_dim(panel_count, narrow_index * group, group)
    block_index = jnp.arange(P_SIZE * B, dtype=jnp.int32) // B
    live = (block_index[None, :] < counts[:, None]).astype(jnp.float32)
    lower_panel = lower_panel * live[:, :, None]

    first, second = pair_lists(P_SIZE)
    npair = len(first)
    blocks = lower_panel.reshape(group, P_SIZE, B, W)
    gram = jnp.einsum("siac,sjbc->sijab", blocks, blocks, precision=lax.Precision.HIGHEST)
    gram = gram.reshape(group, P_SIZE * P_SIZE, B, B)
    contribution = gram[:, first * P_SIZE + second]

    quarters = lax.all_to_all(contribution, "narrow", split_axis=2, concat_axis=0, tiled=True)
    quarter_rows = quarters.shape[2]
    pair_rows = supers_here * npair
    quarters = quarters.reshape(pair_rows, quarter_rows, B)

    capacity = max(2, (pair_rows + wide_count - 1) // wide_count)
    owners = pair_owner[:, 0]
    owner_table = (owners[:, None] == jnp.arange(wide_count, dtype=jnp.int32)[None, :]).astype(
        jnp.int32
    )
    earlier = jnp.cumsum(owner_table, axis=0) - owner_table
    rank_here = jnp.sum(earlier * owner_table, axis=1)
    position = owners * capacity + rank_here
    buffer_rows = wide_count * capacity
    row_slots = T_DEV * narrow_count
    slot_ids = jnp.full((buffer_rows,), -1.0, jnp.float32).at[position].set(
        pair_slot.astype(jnp.float32)
    )
    source_row = jnp.zeros((buffer_rows,), jnp.int32).at[position].set(
        jnp.arange(pair_rows, dtype=jnp.int32)
    )
    filled = jnp.zeros((buffer_rows,), jnp.bool_).at[position].set(True)
    send_buffer = jnp.where(filled[:, None, None], quarters[source_row], 0.0)
    meta = jnp.zeros((wide_count, 8, B), jnp.float32)
    meta = meta.at[:, 0, :capacity].set(slot_ids.reshape(wide_count, capacity))
    send_buffer = jnp.concatenate(
        [send_buffer.reshape(wide_count, capacity * quarter_rows, B), meta], axis=1
    )
    send_buffer, factor, lower_panel = lax.optimization_barrier((send_buffer, factor, lower_panel))
    received = lax.all_to_all(send_buffer, "wide", split_axis=0, concat_axis=0, tiled=True)
    factor_back = columns_out(factor, narrow_count, col_width, 0)
    lower_back = columns_out(lower_panel, narrow_count, col_width, 1)
    received, factor_back, lower_back = lax.optimization_barrier((received, factor_back, lower_back))
    got_slots = received[:, capacity * quarter_rows, :capacity].reshape(buffer_rows)
    got_slots = got_slots.astype(jnp.int32)
    received = received[:, : capacity * quarter_rows, :].reshape(buffer_rows, quarter_rows, B)
    slot_table = (got_slots[:, None] == jnp.arange(row_slots, dtype=jnp.int32)[None, :]).astype(
        jnp.float32
    )
    slot_sums = jnp.einsum("ri,rab->iab", slot_table, received, precision=lax.Precision.HIGHEST)
    slot_sums = slot_sums.reshape(narrow_count, T_DEV, quarter_rows, B)
    summed = lax.all_to_all(slot_sums, "narrow", split_axis=0, concat_axis=2, tiled=True)
    summed = summed.reshape(T_DEV, B, B)
    return (factor_back, lower_back, ancestor - summed)


def solution(mesh):
    placed = (
        P("wide", None, "narrow"),
        P("wide", None, "narrow"),
        P("wide"),
        P("wide", None),
        P("wide"),
        P(("wide", "narrow"), None, None),
    )
    return jax.shard_map(
        local,
        mesh=mesh,
        in_specs=placed,
        out_specs=(
            P("wide", None, "narrow"),
            P("wide", None, "narrow"),
            P(("wide", "narrow"), None, None),
        ),
        check_vma=False,
    )
```

```python
import functools

import jax
import jax.numpy as jnp
import numpy as np
from jax import lax
from jax.experimental import pallas as pl
from jax.experimental.pallas import tpu as pltpu
from jax.sharding import PartitionSpec as P

MESH = pl.DeviceIdType.MESH

W = 512
B = 128
P_SIZE = 8
T_DEV = 2


def pair_lists(count):
    first = []
    second = []
    for outer in range(count):
        for inner in range(outer + 1):
            first.append(outer)
            second.append(inner)
    return (np.array(first, np.int32), np.array(second, np.int32))


def columns_out_kernel(x_ref, y_ref, send_sem, recv_sem, own_sem, *, count, group, width):
    me = lax.axis_index("narrow")
    wide = lax.axis_index("wide")
    barrier = pltpu.get_barrier_semaphore()
    for d in range(1, count):
        peer = lax.rem(me + d, count)
        pl.semaphore_signal(barrier, inc=1, device_id=(wide, peer), device_id_type=MESH)
    pl.semaphore_wait(barrier, count - 1)
    mine = y_ref.at[pl.ds(me * group, group)]
    own = pltpu.make_async_copy(
        x_ref.at[:, :, pl.ds(pl.multiple_of(me * width, width), width)], mine, own_sem
    )
    own.start()
    copies = []
    for d in range(1, count):
        peer = lax.rem(me + d, count)
        copy = pltpu.make_async_remote_copy(
            src_ref=x_ref.at[:, :, pl.ds(pl.multiple_of(peer * width, width), width)],
            dst_ref=mine,
            send_sem=send_sem.at[d - 1],
            recv_sem=recv_sem.at[d - 1],
            device_id=(wide, peer),
            device_id_type=MESH,
        )
        copy.start()
        copies.append(copy)
    own.wait()
    for copy in copies:
        copy.wait()


def columns_out(x, count, width, collective_id):
    group, rows, _ = x.shape
    nbytes = x.size * 4
    return pl.pallas_call(
        functools.partial(columns_out_kernel, count=count, group=group, width=width),
        out_shape=jax.ShapeDtypeStruct((group * count, rows, width), x.dtype),
        in_specs=[pl.BlockSpec(memory_space=pl.ANY)],
        out_specs=pl.BlockSpec(memory_space=pl.ANY),
        scratch_shapes=[
            pltpu.SemaphoreType.DMA((count - 1,)),
            pltpu.SemaphoreType.DMA((count - 1,)),
            pltpu.SemaphoreType.DMA,
        ],
        compiler_params=pltpu.CompilerParams(collective_id=collective_id, has_side_effects=True),
        cost_estimate=pl.CostEstimate(flops=0, bytes_accessed=2 * nbytes, transcendentals=0),
    )(x)


def block_chol_kernel(a_ref, l_ref, inv_ref, work, upper, elim):
    n = a_ref.shape[0]
    phase = 32
    work[...] = a_ref[...]
    rows = lax.broadcasted_iota(jnp.int32, (n, n), 0)
    cols = lax.broadcasted_iota(jnp.int32, (n, n), 1)
    elim[...] = (rows == cols).astype(jnp.float32)
    lane = lax.broadcasted_iota(jnp.int32, (1, n), 1)

    for top in range(0, n, phase):
        height = n - top
        tail_cols = lax.broadcasted_iota(jnp.int32, (height, n), 1)
        tail_rows = top + lax.broadcasted_iota(jnp.int32, (height, 1), 0)

        def step(j, carry, top=top, tail_cols=tail_cols, tail_rows=tail_rows):
            r = work[pl.ds(j, 1), :]
            whole = work[top:, :]
            col = jnp.sum(jnp.where(tail_cols == j, whole, 0.0), axis=1, keepdims=True)
            piv = jnp.sum(jnp.where(lane == j, r, 0.0), axis=1, keepdims=True)
            inv_piv = 1.0 / piv
            r_live = jnp.where(lane >= j, r, 0.0)
            mult = jnp.where(tail_rows > j, col * inv_piv, 0.0)
            work[top:, :] = whole - mult * r_live
            e_row = elim[pl.ds(j, 1), :]
            elim[top:, :] = elim[top:, :] - mult * e_row
            scale = 1.0 / jnp.sqrt(piv)
            upper[pl.ds(j, 1), :] = r_live * scale
            inv_ref[pl.ds(j, 1), :] = e_row * scale
            return carry

        lax.fori_loop(top, top + phase, step, 0)
    l_ref[...] = jnp.transpose(upper[...])


def block_chol(a):
    n = a.shape[-1]
    return pl.pallas_call(
        block_chol_kernel,
        out_shape=(jax.ShapeDtypeStruct((n, n), jnp.float32), jax.ShapeDtypeStruct((n, n), jnp.float32)),
        in_specs=[pl.BlockSpec(memory_space=pltpu.VMEM)],
        out_specs=(pl.BlockSpec(memory_space=pltpu.VMEM), pl.BlockSpec(memory_space=pltpu.VMEM)),
        scratch_shapes=[pltpu.VMEM((n, n), jnp.float32)] * 3,
    )(a)


def chunks_out_kernel(x_ref, y_ref, send_sem, recv_sem, own_sem, *, count):
    me = lax.axis_index("narrow")
    wide = lax.axis_index("wide")
    barrier = pltpu.get_barrier_semaphore()
    for d in range(1, count):
        peer = lax.rem(me + d, count)
        pl.semaphore_signal(barrier, inc=1, device_id=(wide, peer), device_id_type=MESH)
    pl.semaphore_wait(barrier, count - 1)
    own = pltpu.make_async_copy(x_ref.at[me], y_ref.at[me], own_sem)
    own.start()
    copies = []
    for d in range(1, count):
        peer = lax.rem(me + d, count)
        copy = pltpu.make_async_remote_copy(
            src_ref=x_ref.at[peer],
            dst_ref=y_ref.at[me],
            send_sem=send_sem.at[d - 1],
            recv_sem=recv_sem.at[d - 1],
            device_id=(wide, peer),
            device_id_type=MESH,
        )
        copy.start()
        copies.append(copy)
    own.wait()
    for copy in copies:
        copy.wait()


def chunks_out(x, collective_id):
    count = x.shape[0]
    return pl.pallas_call(
        functools.partial(chunks_out_kernel, count=count),
        out_shape=jax.ShapeDtypeStruct(x.shape, x.dtype),
        in_specs=[pl.BlockSpec(memory_space=pl.ANY)],
        out_specs=pl.BlockSpec(memory_space=pl.ANY),
        scratch_shapes=[
            pltpu.SemaphoreType.DMA((count - 1,)),
            pltpu.SemaphoreType.DMA((count - 1,)),
            pltpu.SemaphoreType.DMA,
        ],
        compiler_params=pltpu.CompilerParams(collective_id=collective_id, has_side_effects=True),
        cost_estimate=pl.CostEstimate(flops=0, bytes_accessed=2 * x.size * 4, transcendentals=0),
    )(x)


def mm(a, b):
    return jnp.einsum("sik,skj->sij", a, b, precision=lax.Precision.HIGHEST)


def mm_t(a, b):
    return jnp.einsum("sik,sjk->sij", a, b, precision=lax.Precision.HIGHEST)


def blocked_cholesky(matrix):
    batch, size, _ = matrix.shape
    nblk = size // B
    eye = jnp.broadcast_to(jnp.eye(B, dtype=jnp.float32), (batch, B, B))
    trailing = matrix
    diag_l, diag_inv, below = [], [], []
    inverse_rows = []
    for k in range(nblk):
        head = trailing[:, :B, :B]
        pieces = [block_chol(head[b]) for b in range(batch)]
        l_kk = jnp.stack([p[0] for p in pieces])
        i_kk = jnp.stack([p[1] for p in pieces])
        diag_l.append(l_kk)
        diag_inv.append(i_kk)
        if k > 0:
            left = jnp.concatenate([below[j][:, (k - j - 1) * B:(k - j) * B, :] for j in range(k)], axis=2)
            upper = jnp.concatenate(inverse_rows, axis=1)
            rest = -mm(left, upper)
            rest = jnp.concatenate([rest[:, :, :k * B], eye, rest[:, :, (k + 1) * B:]], axis=2)
            inverse_rows.append(mm(i_kk, rest))
        else:
            inverse_rows.append(jnp.concatenate(
                [i_kk, jnp.zeros((batch, B, size - B), jnp.float32)], axis=2))
        if k < nblk - 1:
            panel_k = mm_t(trailing[:, B:, :B], i_kk)
            below.append(panel_k)
            trailing = trailing[:, B:, B:] - mm_t(panel_k, panel_k)
    columns = []
    for k in range(nblk):
        parts = []
        if k > 0:
            parts.append(jnp.zeros((batch, k * B, B), jnp.float32))
        parts.append(diag_l[k])
        if k < nblk - 1:
            parts.append(below[k])
        columns.append(jnp.concatenate(parts, axis=1))
    factor = jnp.concatenate(columns, axis=2)
    inverse = jnp.concatenate(inverse_rows, axis=1)
    return factor, inverse


def local(diag_block, panel, panel_count, pair_owner, pair_slot, ancestor):
    supers_here = diag_block.shape[0]
    col_width = diag_block.shape[2]
    diag_rows = diag_block.shape[1]
    narrow_index = lax.axis_index("narrow")
    narrow_count = lax.axis_size("narrow")
    wide_count = lax.axis_size("wide")
    group = supers_here // narrow_count

    whole_diag = lax.all_to_all(diag_block, "narrow", split_axis=0, concat_axis=2, tiled=True)
    whole_panel = lax.all_to_all(panel, "narrow", split_axis=0, concat_axis=2, tiled=True)

    factor, inverse = blocked_cholesky(whole_diag)
    lower_panel = jnp.einsum(
        "srk,sck->src", whole_panel, inverse, precision=lax.Precision.HIGHEST
    )
    counts = lax.dynamic_slice_in_dim(panel_count, narrow_index * group, group)
    block_index = jnp.arange(P_SIZE * B, dtype=jnp.int32) // B
    live = (block_index[None, :] < counts[:, None]).astype(jnp.float32)
    lower_panel = lower_panel * live[:, :, None]

    first, second = pair_lists(P_SIZE)
    npair = len(first)
    blocks = lower_panel.reshape(group, P_SIZE, B, W)
    gram = jnp.einsum("siac,sjbc->sijab", blocks, blocks, precision=lax.Precision.HIGHEST)
    gram = gram.reshape(group, P_SIZE * P_SIZE, B, B)
    contribution = gram[:, first * P_SIZE + second]

    quarters = lax.all_to_all(contribution, "narrow", split_axis=2, concat_axis=0, tiled=True)
    quarter_rows = quarters.shape[2]
    pair_rows = supers_here * npair
    quarters = quarters.reshape(pair_rows, quarter_rows, B)

    capacity = max(2, (pair_rows + wide_count - 1) // wide_count)
    owners = pair_owner[:, 0]
    owner_table = (owners[:, None] == jnp.arange(wide_count, dtype=jnp.int32)[None, :]).astype(
        jnp.int32
    )
    earlier = jnp.cumsum(owner_table, axis=0) - owner_table
    rank_here = jnp.sum(earlier * owner_table, axis=1)
    position = owners * capacity + rank_here
    buffer_rows = wide_count * capacity
    row_slots = T_DEV * narrow_count
    slot_ids = jnp.full((buffer_rows,), -1.0, jnp.float32).at[position].set(
        pair_slot.astype(jnp.float32)
    )
    source_row = jnp.zeros((buffer_rows,), jnp.int32).at[position].set(
        jnp.arange(pair_rows, dtype=jnp.int32)
    )
    filled = jnp.zeros((buffer_rows,), jnp.bool_).at[position].set(True)
    send_buffer = jnp.where(filled[:, None, None], quarters[source_row], 0.0)
    meta = jnp.zeros((wide_count, 8, B), jnp.float32)
    meta = meta.at[:, 0, :capacity].set(slot_ids.reshape(wide_count, capacity))
    send_buffer = jnp.concatenate(
        [send_buffer.reshape(wide_count, capacity * quarter_rows, B), meta], axis=1
    )
    send_buffer, factor, lower_panel = lax.optimization_barrier((send_buffer, factor, lower_panel))
    received = lax.all_to_all(send_buffer, "wide", split_axis=0, concat_axis=0, tiled=True)
    factor_back = columns_out(factor, narrow_count, col_width, 0)
    lower_back = columns_out(lower_panel, narrow_count, col_width, 1)
    received, factor_back, lower_back = lax.optimization_barrier((received, factor_back, lower_back))
    got_slots = received[:, capacity * quarter_rows, :capacity].reshape(buffer_rows)
    got_slots = got_slots.astype(jnp.int32)
    received = received[:, : capacity * quarter_rows, :].reshape(buffer_rows, quarter_rows, B)
    slot_table = (got_slots[:, None] == jnp.arange(row_slots, dtype=jnp.int32)[None, :]).astype(
        jnp.float32
    )
    slot_sums = jnp.einsum("ri,rab->iab", slot_table, received, precision=lax.Precision.HIGHEST)
    slot_sums = slot_sums.reshape(narrow_count, T_DEV, quarter_rows, B)
    arrived = chunks_out(slot_sums, 2)
    summed = jnp.swapaxes(arrived, 0, 1).reshape(T_DEV, B, B)
    return (factor_back, lower_back, ancestor - summed)


def solution(mesh):
    placed = (
        P("wide", None, "narrow"),
        P("wide", None, "narrow"),
        P("wide"),
        P("wide", None),
        P("wide"),
        P(("wide", "narrow"), None, None),
    )
    return jax.shard_map(
        local,
        mesh=mesh,
        in_specs=placed,
        out_specs=(
            P("wide", None, "narrow"),
            P("wide", None, "narrow"),
            P(("wide", "narrow"), None, None),
        ),
        check_vma=False,
    )
```

```python
import functools

import jax
import jax.numpy as jnp
import numpy as np
from jax import lax
from jax.experimental import pallas as pl
from jax.experimental.pallas import tpu as pltpu
from jax.sharding import PartitionSpec as P

MESH = pl.DeviceIdType.MESH

W = 512
B = 128
P_SIZE = 8
T_DEV = 2


def pair_lists(count):
    first = []
    second = []
    for outer in range(count):
        for inner in range(outer + 1):
            first.append(outer)
            second.append(inner)
    return (np.array(first, np.int32), np.array(second, np.int32))


def columns_out_kernel(x_ref, y_ref, send_sem, recv_sem, own_sem, *, count, group, width):
    me = lax.axis_index("narrow")
    wide = lax.axis_index("wide")
    barrier = pltpu.get_barrier_semaphore()
    for d in range(1, count):
        peer = lax.rem(me + d, count)
        pl.semaphore_signal(barrier, inc=1, device_id=(wide, peer), device_id_type=MESH)
    pl.semaphore_wait(barrier, count - 1)
    mine = y_ref.at[pl.ds(me * group, group)]
    own = pltpu.make_async_copy(
        x_ref.at[:, :, pl.ds(pl.multiple_of(me * width, width), width)], mine, own_sem
    )
    own.start()
    copies = []
    for d in range(1, count):
        peer = lax.rem(me + d, count)
        copy = pltpu.make_async_remote_copy(
            src_ref=x_ref.at[:, :, pl.ds(pl.multiple_of(peer * width, width), width)],
            dst_ref=mine,
            send_sem=send_sem.at[d - 1],
            recv_sem=recv_sem.at[d - 1],
            device_id=(wide, peer),
            device_id_type=MESH,
        )
        copy.start()
        copies.append(copy)
    own.wait()
    for copy in copies:
        copy.wait()


def columns_out(x, count, width, collective_id):
    group, rows, _ = x.shape
    nbytes = x.size * 4
    return pl.pallas_call(
        functools.partial(columns_out_kernel, count=count, group=group, width=width),
        out_shape=jax.ShapeDtypeStruct((group * count, rows, width), x.dtype),
        in_specs=[pl.BlockSpec(memory_space=pl.ANY)],
        out_specs=pl.BlockSpec(memory_space=pl.ANY),
        scratch_shapes=[
            pltpu.SemaphoreType.DMA((count - 1,)),
            pltpu.SemaphoreType.DMA((count - 1,)),
            pltpu.SemaphoreType.DMA,
        ],
        compiler_params=pltpu.CompilerParams(collective_id=collective_id, has_side_effects=True),
        cost_estimate=pl.CostEstimate(flops=0, bytes_accessed=2 * nbytes, transcendentals=0),
    )(x)


def block_chol_kernel(a_ref, l_ref, inv_ref, work, upper, elim):
    n = a_ref.shape[0]
    phase = 32
    work[...] = a_ref[...]
    rows = lax.broadcasted_iota(jnp.int32, (n, n), 0)
    cols = lax.broadcasted_iota(jnp.int32, (n, n), 1)
    elim[...] = (rows == cols).astype(jnp.float32)
    lane = lax.broadcasted_iota(jnp.int32, (1, n), 1)

    for top in range(0, n, phase):
        height = n - top
        tail_cols = lax.broadcasted_iota(jnp.int32, (height, n), 1)
        tail_rows = top + lax.broadcasted_iota(jnp.int32, (height, 1), 0)

        def step(j, carry, top=top, tail_cols=tail_cols, tail_rows=tail_rows):
            r = work[pl.ds(j, 1), :]
            whole = work[top:, :]
            col = jnp.sum(jnp.where(tail_cols == j, whole, 0.0), axis=1, keepdims=True)
            piv = jnp.sum(jnp.where(lane == j, r, 0.0), axis=1, keepdims=True)
            inv_piv = 1.0 / piv
            r_live = jnp.where(lane >= j, r, 0.0)
            mult = jnp.where(tail_rows > j, col * inv_piv, 0.0)
            work[top:, :] = whole - mult * r_live
            e_row = elim[pl.ds(j, 1), :]
            elim[top:, :] = elim[top:, :] - mult * e_row
            scale = 1.0 / jnp.sqrt(piv)
            upper[pl.ds(j, 1), :] = r_live * scale
            inv_ref[pl.ds(j, 1), :] = e_row * scale
            return carry

        lax.fori_loop(top, top + phase, step, 0)
    l_ref[...] = jnp.transpose(upper[...])


def block_chol(a):
    n = a.shape[-1]
    return pl.pallas_call(
        block_chol_kernel,
        out_shape=(jax.ShapeDtypeStruct((n, n), jnp.float32), jax.ShapeDtypeStruct((n, n), jnp.float32)),
        in_specs=[pl.BlockSpec(memory_space=pltpu.VMEM)],
        out_specs=(pl.BlockSpec(memory_space=pltpu.VMEM), pl.BlockSpec(memory_space=pltpu.VMEM)),
        scratch_shapes=[pltpu.VMEM((n, n), jnp.float32)] * 3,
    )(a)


def chunks_out_kernel(x_ref, y_ref, send_sem, recv_sem, own_sem, *, count):
    me = lax.axis_index("narrow")
    wide = lax.axis_index("wide")
    barrier = pltpu.get_barrier_semaphore()
    for d in range(1, count):
        peer = lax.rem(me + d, count)
        pl.semaphore_signal(barrier, inc=1, device_id=(wide, peer), device_id_type=MESH)
    pl.semaphore_wait(barrier, count - 1)
    own = pltpu.make_async_copy(x_ref.at[me], y_ref.at[me], own_sem)
    own.start()
    copies = []
    for d in range(1, count):
        peer = lax.rem(me + d, count)
        copy = pltpu.make_async_remote_copy(
            src_ref=x_ref.at[peer],
            dst_ref=y_ref.at[me],
            send_sem=send_sem.at[d - 1],
            recv_sem=recv_sem.at[d - 1],
            device_id=(wide, peer),
            device_id_type=MESH,
        )
        copy.start()
        copies.append(copy)
    own.wait()
    for copy in copies:
        copy.wait()


def chunks_out(x, collective_id):
    count = x.shape[0]
    return pl.pallas_call(
        functools.partial(chunks_out_kernel, count=count),
        out_shape=jax.ShapeDtypeStruct(x.shape, x.dtype),
        in_specs=[pl.BlockSpec(memory_space=pl.ANY)],
        out_specs=pl.BlockSpec(memory_space=pl.ANY),
        scratch_shapes=[
            pltpu.SemaphoreType.DMA((count - 1,)),
            pltpu.SemaphoreType.DMA((count - 1,)),
            pltpu.SemaphoreType.DMA,
        ],
        compiler_params=pltpu.CompilerParams(collective_id=collective_id, has_side_effects=True),
        cost_estimate=pl.CostEstimate(flops=0, bytes_accessed=2 * x.size * 4, transcendentals=0),
    )(x)


def quarters_out_kernel(x_ref, y_ref, send_sem, recv_sem, own_sem, *, count, group, height):
    me = lax.axis_index("narrow")
    wide = lax.axis_index("wide")
    barrier = pltpu.get_barrier_semaphore()
    for d in range(1, count):
        peer = lax.rem(me + d, count)
        pl.semaphore_signal(barrier, inc=1, device_id=(wide, peer), device_id_type=MESH)
    pl.semaphore_wait(barrier, count - 1)
    mine = y_ref.at[pl.ds(me * group, group)]
    own = pltpu.make_async_copy(
        x_ref.at[:, :, pl.ds(pl.multiple_of(me * height, height), height), :], mine, own_sem
    )
    own.start()
    copies = []
    for d in range(1, count):
        peer = lax.rem(me + d, count)
        copy = pltpu.make_async_remote_copy(
            src_ref=x_ref.at[:, :, pl.ds(pl.multiple_of(peer * height, height), height), :],
            dst_ref=mine,
            send_sem=send_sem.at[d - 1],
            recv_sem=recv_sem.at[d - 1],
            device_id=(wide, peer),
            device_id_type=MESH,
        )
        copy.start()
        copies.append(copy)
    own.wait()
    for copy in copies:
        copy.wait()


def quarters_out(x, count, collective_id):
    group, pairs, rows, width = x.shape
    height = rows // count
    return pl.pallas_call(
        functools.partial(quarters_out_kernel, count=count, group=group, height=height),
        out_shape=jax.ShapeDtypeStruct((group * count, pairs, height, width), x.dtype),
        in_specs=[pl.BlockSpec(memory_space=pl.ANY)],
        out_specs=pl.BlockSpec(memory_space=pl.ANY),
        scratch_shapes=[
            pltpu.SemaphoreType.DMA((count - 1,)),
            pltpu.SemaphoreType.DMA((count - 1,)),
            pltpu.SemaphoreType.DMA,
        ],
        compiler_params=pltpu.CompilerParams(collective_id=collective_id, has_side_effects=True),
        cost_estimate=pl.CostEstimate(flops=0, bytes_accessed=2 * x.size * 4, transcendentals=0),
    )(x)


def mm(a, b):
    return jnp.einsum("sik,skj->sij", a, b, precision=lax.Precision.HIGHEST)


def mm_t(a, b):
    return jnp.einsum("sik,sjk->sij", a, b, precision=lax.Precision.HIGHEST)


def blocked_cholesky(matrix):
    batch, size, _ = matrix.shape
    nblk = size // B
    eye = jnp.broadcast_to(jnp.eye(B, dtype=jnp.float32), (batch, B, B))
    trailing = matrix
    diag_l, diag_inv, below = [], [], []
    inverse_rows = []
    for k in range(nblk):
        head = trailing[:, :B, :B]
        pieces = [block_chol(head[b]) for b in range(batch)]
        l_kk = jnp.stack([p[0] for p in pieces])
        i_kk = jnp.stack([p[1] for p in pieces])
        diag_l.append(l_kk)
        diag_inv.append(i_kk)
        if k > 0:
            left = jnp.concatenate([below[j][:, (k - j - 1) * B:(k - j) * B, :] for j in range(k)], axis=2)
            upper = jnp.concatenate(inverse_rows, axis=1)
            rest = -mm(left, upper)
            rest = jnp.concatenate([rest[:, :, :k * B], eye, rest[:, :, (k + 1) * B:]], axis=2)
            inverse_rows.append(mm(i_kk, rest))
        else:
            inverse_rows.append(jnp.concatenate(
                [i_kk, jnp.zeros((batch, B, size - B), jnp.float32)], axis=2))
        if k < nblk - 1:
            panel_k = mm_t(trailing[:, B:, :B], i_kk)
            below.append(panel_k)
            trailing = trailing[:, B:, B:] - mm_t(panel_k, panel_k)
    columns = []
    for k in range(nblk):
        parts = []
        if k > 0:
            parts.append(jnp.zeros((batch, k * B, B), jnp.float32))
        parts.append(diag_l[k])
        if k < nblk - 1:
            parts.append(below[k])
        columns.append(jnp.concatenate(parts, axis=1))
    factor = jnp.concatenate(columns, axis=2)
    inverse = jnp.concatenate(inverse_rows, axis=1)
    return factor, inverse


def local(diag_block, panel, panel_count, pair_owner, pair_slot, ancestor):
    supers_here = diag_block.shape[0]
    col_width = diag_block.shape[2]
    diag_rows = diag_block.shape[1]
    narrow_index = lax.axis_index("narrow")
    narrow_count = lax.axis_size("narrow")
    wide_count = lax.axis_size("wide")
    group = supers_here // narrow_count

    whole_diag = lax.all_to_all(diag_block, "narrow", split_axis=0, concat_axis=2, tiled=True)
    whole_panel = lax.all_to_all(panel, "narrow", split_axis=0, concat_axis=2, tiled=True)

    factor, inverse = blocked_cholesky(whole_diag)
    lower_panel = jnp.einsum(
        "srk,sck->src", whole_panel, inverse, precision=lax.Precision.HIGHEST
    )
    counts = lax.dynamic_slice_in_dim(panel_count, narrow_index * group, group)
    block_index = jnp.arange(P_SIZE * B, dtype=jnp.int32) // B
    live = (block_index[None, :] < counts[:, None]).astype(jnp.float32)
    lower_panel = lower_panel * live[:, :, None]

    first, second = pair_lists(P_SIZE)
    npair = len(first)
    blocks = lower_panel.reshape(group, P_SIZE, B, W)
    gram = jnp.einsum("siac,sjbc->sijab", blocks, blocks, precision=lax.Precision.HIGHEST)
    gram = gram.reshape(group, P_SIZE * P_SIZE, B, B)
    contribution = gram[:, first * P_SIZE + second]

    quarters = quarters_out(contribution, narrow_count, 3)
    quarter_rows = quarters.shape[2]
    pair_rows = supers_here * npair
    quarters = quarters.reshape(pair_rows, quarter_rows, B)

    capacity = max(2, (pair_rows + wide_count - 1) // wide_count)
    owners = pair_owner[:, 0]
    owner_table = (owners[:, None] == jnp.arange(wide_count, dtype=jnp.int32)[None, :]).astype(
        jnp.int32
    )
    earlier = jnp.cumsum(owner_table, axis=0) - owner_table
    rank_here = jnp.sum(earlier * owner_table, axis=1)
    position = owners * capacity + rank_here
    buffer_rows = wide_count * capacity
    row_slots = T_DEV * narrow_count
    slot_ids = jnp.full((buffer_rows,), -1.0, jnp.float32).at[position].set(
        pair_slot.astype(jnp.float32)
    )
    source_row = jnp.zeros((buffer_rows,), jnp.int32).at[position].set(
        jnp.arange(pair_rows, dtype=jnp.int32)
    )
    filled = jnp.zeros((buffer_rows,), jnp.bool_).at[position].set(True)
    send_buffer = jnp.where(filled[:, None, None], quarters[source_row], 0.0)
    meta = jnp.zeros((wide_count, 8, B), jnp.float32)
    meta = meta.at[:, 0, :capacity].set(slot_ids.reshape(wide_count, capacity))
    send_buffer = jnp.concatenate(
        [send_buffer.reshape(wide_count, capacity * quarter_rows, B), meta], axis=1
    )
    send_buffer, factor, lower_panel = lax.optimization_barrier((send_buffer, factor, lower_panel))
    received = lax.all_to_all(send_buffer, "wide", split_axis=0, concat_axis=0, tiled=True)
    factor_back = columns_out(factor, narrow_count, col_width, 0)
    lower_back = columns_out(lower_panel, narrow_count, col_width, 1)
    received, factor_back, lower_back = lax.optimization_barrier((received, factor_back, lower_back))
    got_slots = received[:, capacity * quarter_rows, :capacity].reshape(buffer_rows)
    got_slots = got_slots.astype(jnp.int32)
    received = received[:, : capacity * quarter_rows, :].reshape(buffer_rows, quarter_rows, B)
    slot_table = (got_slots[:, None] == jnp.arange(row_slots, dtype=jnp.int32)[None, :]).astype(
        jnp.float32
    )
    slot_sums = jnp.einsum("ri,rab->iab", slot_table, received, precision=lax.Precision.HIGHEST)
    slot_sums = slot_sums.reshape(narrow_count, T_DEV, quarter_rows, B)
    arrived = chunks_out(slot_sums, 2)
    summed = jnp.swapaxes(arrived, 0, 1).reshape(T_DEV, B, B)
    return (factor_back, lower_back, ancestor - summed)


def solution(mesh):
    placed = (
        P("wide", None, "narrow"),
        P("wide", None, "narrow"),
        P("wide"),
        P("wide", None),
        P("wide"),
        P(("wide", "narrow"), None, None),
    )
    return jax.shard_map(
        local,
        mesh=mesh,
        in_specs=placed,
        out_specs=(
            P("wide", None, "narrow"),
            P("wide", None, "narrow"),
            P(("wide", "narrow"), None, None),
        ),
        check_vma=False,
    )
```

```python
import functools

import jax
import jax.numpy as jnp
import numpy as np
from jax import lax
from jax.experimental import pallas as pl
from jax.experimental.pallas import tpu as pltpu
from jax.sharding import PartitionSpec as P

MESH = pl.DeviceIdType.MESH

W = 512
B = 128
P_SIZE = 8
T_DEV = 2


def pair_lists(count):
    first = []
    second = []
    for outer in range(count):
        for inner in range(outer + 1):
            first.append(outer)
            second.append(inner)
    return (np.array(first, np.int32), np.array(second, np.int32))


def columns_out_kernel(x_ref, y_ref, send_sem, recv_sem, own_sem, *, count, group, width):
    me = lax.axis_index("narrow")
    wide = lax.axis_index("wide")
    barrier = pltpu.get_barrier_semaphore()
    for d in range(1, count):
        peer = lax.rem(me + d, count)
        pl.semaphore_signal(barrier, inc=1, device_id=(wide, peer), device_id_type=MESH)
    pl.semaphore_wait(barrier, count - 1)
    mine = y_ref.at[pl.ds(me * group, group)]
    own = pltpu.make_async_copy(
        x_ref.at[:, :, pl.ds(pl.multiple_of(me * width, width), width)], mine, own_sem
    )
    own.start()
    copies = []
    for d in range(1, count):
        peer = lax.rem(me + d, count)
        copy = pltpu.make_async_remote_copy(
            src_ref=x_ref.at[:, :, pl.ds(pl.multiple_of(peer * width, width), width)],
            dst_ref=mine,
            send_sem=send_sem.at[d - 1],
            recv_sem=recv_sem.at[d - 1],
            device_id=(wide, peer),
            device_id_type=MESH,
        )
        copy.start()
        copies.append(copy)
    own.wait()
    for copy in copies:
        copy.wait()


def columns_out(x, count, width, collective_id):
    group, rows, _ = x.shape
    nbytes = x.size * 4
    return pl.pallas_call(
        functools.partial(columns_out_kernel, count=count, group=group, width=width),
        out_shape=jax.ShapeDtypeStruct((group * count, rows, width), x.dtype),
        in_specs=[pl.BlockSpec(memory_space=pl.ANY)],
        out_specs=pl.BlockSpec(memory_space=pl.ANY),
        scratch_shapes=[
            pltpu.SemaphoreType.DMA((count - 1,)),
            pltpu.SemaphoreType.DMA((count - 1,)),
            pltpu.SemaphoreType.DMA,
        ],
        compiler_params=pltpu.CompilerParams(collective_id=collective_id, has_side_effects=True),
        cost_estimate=pl.CostEstimate(flops=0, bytes_accessed=2 * nbytes, transcendentals=0),
    )(x)


def block_chol_kernel(a_ref, l_ref, inv_ref, work, upper, elim):
    n = a_ref.shape[0]
    phase = 32
    work[...] = a_ref[...]
    rows = lax.broadcasted_iota(jnp.int32, (n, n), 0)
    cols = lax.broadcasted_iota(jnp.int32, (n, n), 1)
    elim[...] = (rows == cols).astype(jnp.float32)
    lane = lax.broadcasted_iota(jnp.int32, (1, n), 1)

    for top in range(0, n, phase):
        height = n - top
        tail_cols = lax.broadcasted_iota(jnp.int32, (height, n), 1)
        tail_rows = top + lax.broadcasted_iota(jnp.int32, (height, 1), 0)

        def step(j, carry, top=top, tail_cols=tail_cols, tail_rows=tail_rows):
            r = work[pl.ds(j, 1), :]
            whole = work[top:, :]
            col = jnp.sum(jnp.where(tail_cols == j, whole, 0.0), axis=1, keepdims=True)
            piv = jnp.sum(jnp.where(lane == j, r, 0.0), axis=1, keepdims=True)
            inv_piv = 1.0 / piv
            r_live = jnp.where(lane >= j, r, 0.0)
            mult = jnp.where(tail_rows > j, col * inv_piv, 0.0)
            work[top:, :] = whole - mult * r_live
            e_row = elim[pl.ds(j, 1), :]
            elim[top:, :] = elim[top:, :] - mult * e_row
            scale = 1.0 / jnp.sqrt(piv)
            upper[pl.ds(j, 1), :] = r_live * scale
            inv_ref[pl.ds(j, 1), :] = e_row * scale
            return carry

        lax.fori_loop(top, top + phase, step, 0)
    l_ref[...] = jnp.transpose(upper[...])


def block_chol(a):
    n = a.shape[-1]
    return pl.pallas_call(
        block_chol_kernel,
        out_shape=(jax.ShapeDtypeStruct((n, n), jnp.float32), jax.ShapeDtypeStruct((n, n), jnp.float32)),
        in_specs=[pl.BlockSpec(memory_space=pltpu.VMEM)],
        out_specs=(pl.BlockSpec(memory_space=pltpu.VMEM), pl.BlockSpec(memory_space=pltpu.VMEM)),
        scratch_shapes=[pltpu.VMEM((n, n), jnp.float32)] * 3,
    )(a)


def chunks_out_kernel(x_ref, y_ref, send_sem, recv_sem, own_sem, *, count):
    me = lax.axis_index("narrow")
    wide = lax.axis_index("wide")
    barrier = pltpu.get_barrier_semaphore()
    for d in range(1, count):
        peer = lax.rem(me + d, count)
        pl.semaphore_signal(barrier, inc=1, device_id=(wide, peer), device_id_type=MESH)
    pl.semaphore_wait(barrier, count - 1)
    own = pltpu.make_async_copy(x_ref.at[me], y_ref.at[me], own_sem)
    own.start()
    copies = []
    for d in range(1, count):
        peer = lax.rem(me + d, count)
        copy = pltpu.make_async_remote_copy(
            src_ref=x_ref.at[peer],
            dst_ref=y_ref.at[me],
            send_sem=send_sem.at[d - 1],
            recv_sem=recv_sem.at[d - 1],
            device_id=(wide, peer),
            device_id_type=MESH,
        )
        copy.start()
        copies.append(copy)
    own.wait()
    for copy in copies:
        copy.wait()


def chunks_out(x, collective_id):
    count = x.shape[0]
    return pl.pallas_call(
        functools.partial(chunks_out_kernel, count=count),
        out_shape=jax.ShapeDtypeStruct(x.shape, x.dtype),
        in_specs=[pl.BlockSpec(memory_space=pl.ANY)],
        out_specs=pl.BlockSpec(memory_space=pl.ANY),
        scratch_shapes=[
            pltpu.SemaphoreType.DMA((count - 1,)),
            pltpu.SemaphoreType.DMA((count - 1,)),
            pltpu.SemaphoreType.DMA,
        ],
        compiler_params=pltpu.CompilerParams(collective_id=collective_id, has_side_effects=True),
        cost_estimate=pl.CostEstimate(flops=0, bytes_accessed=2 * x.size * 4, transcendentals=0),
    )(x)


def quarters_out_kernel(x_ref, y_ref, send_sem, recv_sem, own_sem, *, count, group, height):
    me = lax.axis_index("narrow")
    wide = lax.axis_index("wide")
    barrier = pltpu.get_barrier_semaphore()
    for d in range(1, count):
        peer = lax.rem(me + d, count)
        pl.semaphore_signal(barrier, inc=1, device_id=(wide, peer), device_id_type=MESH)
    pl.semaphore_wait(barrier, count - 1)
    mine = y_ref.at[pl.ds(me * group, group)]
    own = pltpu.make_async_copy(
        x_ref.at[:, :, pl.ds(pl.multiple_of(me * height, height), height), :], mine, own_sem
    )
    own.start()
    copies = []
    for d in range(1, count):
        peer = lax.rem(me + d, count)
        copy = pltpu.make_async_remote_copy(
            src_ref=x_ref.at[:, :, pl.ds(pl.multiple_of(peer * height, height), height), :],
            dst_ref=mine,
            send_sem=send_sem.at[d - 1],
            recv_sem=recv_sem.at[d - 1],
            device_id=(wide, peer),
            device_id_type=MESH,
        )
        copy.start()
        copies.append(copy)
    own.wait()
    for copy in copies:
        copy.wait()


def quarters_out(x, count, collective_id):
    group, pairs, rows, width = x.shape
    height = rows // count
    return pl.pallas_call(
        functools.partial(quarters_out_kernel, count=count, group=group, height=height),
        out_shape=jax.ShapeDtypeStruct((group * count, pairs, height, width), x.dtype),
        in_specs=[pl.BlockSpec(memory_space=pl.ANY)],
        out_specs=pl.BlockSpec(memory_space=pl.ANY),
        scratch_shapes=[
            pltpu.SemaphoreType.DMA((count - 1,)),
            pltpu.SemaphoreType.DMA((count - 1,)),
            pltpu.SemaphoreType.DMA,
        ],
        compiler_params=pltpu.CompilerParams(collective_id=collective_id, has_side_effects=True),
        cost_estimate=pl.CostEstimate(flops=0, bytes_accessed=2 * x.size * 4, transcendentals=0),
    )(x)


def mm(a, b):
    return jnp.einsum("sik,skj->sij", a, b, precision=lax.Precision.HIGHEST)


def mm_t(a, b):
    return jnp.einsum("sik,sjk->sij", a, b, precision=lax.Precision.HIGHEST)


def blocked_cholesky(matrix):
    batch, size, _ = matrix.shape
    nblk = size // B
    eye = jnp.broadcast_to(jnp.eye(B, dtype=jnp.float32), (batch, B, B))
    trailing = matrix
    diag_l, diag_inv, below = [], [], []
    inverse_rows = []
    for k in range(nblk):
        head = trailing[:, :B, :B]
        pieces = [block_chol(head[b]) for b in range(batch)]
        l_kk = jnp.stack([p[0] for p in pieces])
        i_kk = jnp.stack([p[1] for p in pieces])
        diag_l.append(l_kk)
        diag_inv.append(i_kk)
        if k > 0:
            left = jnp.concatenate([below[j][:, (k - j - 1) * B:(k - j) * B, :] for j in range(k)], axis=2)
            upper = jnp.concatenate(inverse_rows, axis=1)
            rest = -mm(left, upper)
            rest = jnp.concatenate([rest[:, :, :k * B], eye, rest[:, :, (k + 1) * B:]], axis=2)
            inverse_rows.append(mm(i_kk, rest))
        else:
            inverse_rows.append(jnp.concatenate(
                [i_kk, jnp.zeros((batch, B, size - B), jnp.float32)], axis=2))
        if k < nblk - 1:
            panel_k = mm_t(trailing[:, B:, :B], i_kk)
            below.append(panel_k)
            trailing = trailing[:, B:, B:] - mm_t(panel_k, panel_k)
    columns = []
    for k in range(nblk):
        parts = []
        if k > 0:
            parts.append(jnp.zeros((batch, k * B, B), jnp.float32))
        parts.append(diag_l[k])
        if k < nblk - 1:
            parts.append(below[k])
        columns.append(jnp.concatenate(parts, axis=1))
    factor = jnp.concatenate(columns, axis=2)
    inverse = jnp.concatenate(inverse_rows, axis=1)
    return factor, inverse


def local(diag_block, panel, panel_count, pair_owner, pair_slot, ancestor):
    supers_here = diag_block.shape[0]
    col_width = diag_block.shape[2]
    diag_rows = diag_block.shape[1]
    narrow_index = lax.axis_index("narrow")
    narrow_count = lax.axis_size("narrow")
    wide_count = lax.axis_size("wide")
    group = supers_here // narrow_count

    whole_diag = lax.all_to_all(diag_block, "narrow", split_axis=0, concat_axis=2, tiled=True)
    whole_panel = lax.all_to_all(panel, "narrow", split_axis=0, concat_axis=2, tiled=True)

    factor, inverse = blocked_cholesky(whole_diag)
    lower_panel = jnp.einsum(
        "srk,sck->src", whole_panel, inverse, precision=lax.Precision.HIGHEST
    )
    counts = lax.dynamic_slice_in_dim(panel_count, narrow_index * group, group)
    block_index = jnp.arange(P_SIZE * B, dtype=jnp.int32) // B
    live = (block_index[None, :] < counts[:, None]).astype(jnp.float32)
    lower_panel = lower_panel * live[:, :, None]

    first, second = pair_lists(P_SIZE)
    npair = len(first)
    blocks = lower_panel.reshape(group, P_SIZE, B, W)
    gram = jnp.einsum("sxc,syc->sxy", lower_panel, lower_panel, precision=lax.Precision.HIGHEST)
    gram = gram.reshape(group, P_SIZE, B, P_SIZE, B)
    contribution = jnp.moveaxis(gram[:, first, :, second, :], 0, 1)

    quarters = quarters_out(contribution, narrow_count, 3)
    quarter_rows = quarters.shape[2]
    pair_rows = supers_here * npair
    quarters = quarters.reshape(pair_rows, quarter_rows, B)

    capacity = max(2, (pair_rows + wide_count - 1) // wide_count)
    owners = pair_owner[:, 0]
    owner_table = (owners[:, None] == jnp.arange(wide_count, dtype=jnp.int32)[None, :]).astype(
        jnp.int32
    )
    earlier = jnp.cumsum(owner_table, axis=0) - owner_table
    rank_here = jnp.sum(earlier * owner_table, axis=1)
    position = owners * capacity + rank_here
    buffer_rows = wide_count * capacity
    row_slots = T_DEV * narrow_count
    slot_ids = jnp.full((buffer_rows,), -1.0, jnp.float32).at[position].set(
        pair_slot.astype(jnp.float32)
    )
    source_row = jnp.zeros((buffer_rows,), jnp.int32).at[position].set(
        jnp.arange(pair_rows, dtype=jnp.int32)
    )
    filled = jnp.zeros((buffer_rows,), jnp.bool_).at[position].set(True)
    send_buffer = jnp.where(filled[:, None, None], quarters[source_row], 0.0)
    meta = jnp.zeros((wide_count, 8, B), jnp.float32)
    meta = meta.at[:, 0, :capacity].set(slot_ids.reshape(wide_count, capacity))
    send_buffer = jnp.concatenate(
        [send_buffer.reshape(wide_count, capacity * quarter_rows, B), meta], axis=1
    )
    send_buffer, factor, lower_panel = lax.optimization_barrier((send_buffer, factor, lower_panel))
    received = lax.all_to_all(send_buffer, "wide", split_axis=0, concat_axis=0, tiled=True)
    factor_back = columns_out(factor, narrow_count, col_width, 0)
    lower_back = columns_out(lower_panel, narrow_count, col_width, 1)
    received, factor_back, lower_back = lax.optimization_barrier((received, factor_back, lower_back))
    got_slots = received[:, capacity * quarter_rows, :capacity].reshape(buffer_rows)
    got_slots = got_slots.astype(jnp.int32)
    received = received[:, : capacity * quarter_rows, :].reshape(buffer_rows, quarter_rows, B)
    slot_table = (got_slots[:, None] == jnp.arange(row_slots, dtype=jnp.int32)[None, :]).astype(
        jnp.float32
    )
    slot_sums = jnp.einsum("ri,rab->iab", slot_table, received, precision=lax.Precision.HIGHEST)
    slot_sums = slot_sums.reshape(narrow_count, T_DEV, quarter_rows, B)
    arrived = chunks_out(slot_sums, 2)
    summed = jnp.swapaxes(arrived, 0, 1).reshape(T_DEV, B, B)
    return (factor_back, lower_back, ancestor - summed)


def solution(mesh):
    placed = (
        P("wide", None, "narrow"),
        P("wide", None, "narrow"),
        P("wide"),
        P("wide", None),
        P("wide"),
        P(("wide", "narrow"), None, None),
    )
    return jax.shard_map(
        local,
        mesh=mesh,
        in_specs=placed,
        out_specs=(
            P("wide", None, "narrow"),
            P("wide", None, "narrow"),
            P(("wide", "narrow"), None, None),
        ),
        check_vma=False,
    )
```

```python
import functools

import jax
import jax.numpy as jnp
import numpy as np
from jax import lax
from jax.experimental import pallas as pl
from jax.experimental.pallas import tpu as pltpu
from jax.sharding import PartitionSpec as P

MESH = pl.DeviceIdType.MESH

W = 512
B = 128
P_SIZE = 8
T_DEV = 2


def pair_lists(count):
    first = []
    second = []
    for outer in range(count):
        for inner in range(outer + 1):
            first.append(outer)
            second.append(inner)
    return (np.array(first, np.int32), np.array(second, np.int32))


def columns_out_kernel(x_ref, y_ref, send_sem, recv_sem, own_sem, *, count, group, width):
    me = lax.axis_index("narrow")
    wide = lax.axis_index("wide")
    barrier = pltpu.get_barrier_semaphore()
    for d in range(1, count):
        peer = lax.rem(me + d, count)
        pl.semaphore_signal(barrier, inc=1, device_id=(wide, peer), device_id_type=MESH)
    pl.semaphore_wait(barrier, count - 1)
    mine = y_ref.at[pl.ds(me * group, group)]
    own = pltpu.make_async_copy(
        x_ref.at[:, :, pl.ds(pl.multiple_of(me * width, width), width)], mine, own_sem
    )
    own.start()
    copies = []
    for d in range(1, count):
        peer = lax.rem(me + d, count)
        copy = pltpu.make_async_remote_copy(
            src_ref=x_ref.at[:, :, pl.ds(pl.multiple_of(peer * width, width), width)],
            dst_ref=mine,
            send_sem=send_sem.at[d - 1],
            recv_sem=recv_sem.at[d - 1],
            device_id=(wide, peer),
            device_id_type=MESH,
        )
        copy.start()
        copies.append(copy)
    own.wait()
    for copy in copies:
        copy.wait()


def columns_out(x, count, width, collective_id):
    group, rows, _ = x.shape
    nbytes = x.size * 4
    return pl.pallas_call(
        functools.partial(columns_out_kernel, count=count, group=group, width=width),
        out_shape=jax.ShapeDtypeStruct((group * count, rows, width), x.dtype),
        in_specs=[pl.BlockSpec(memory_space=pl.ANY)],
        out_specs=pl.BlockSpec(memory_space=pl.ANY),
        scratch_shapes=[
            pltpu.SemaphoreType.DMA((count - 1,)),
            pltpu.SemaphoreType.DMA((count - 1,)),
            pltpu.SemaphoreType.DMA,
        ],
        compiler_params=pltpu.CompilerParams(collective_id=collective_id, has_side_effects=True),
        cost_estimate=pl.CostEstimate(flops=0, bytes_accessed=2 * nbytes, transcendentals=0),
    )(x)


def block_chol_kernel(a_ref, l_ref, inv_ref, work, upper, elim):
    n = a_ref.shape[0]
    phase = 32
    work[...] = a_ref[...]
    rows = lax.broadcasted_iota(jnp.int32, (n, n), 0)
    cols = lax.broadcasted_iota(jnp.int32, (n, n), 1)
    elim[...] = (rows == cols).astype(jnp.float32)
    lane = lax.broadcasted_iota(jnp.int32, (1, n), 1)

    for top in range(0, n, phase):
        height = n - top
        tail_cols = lax.broadcasted_iota(jnp.int32, (height, n), 1)
        tail_rows = top + lax.broadcasted_iota(jnp.int32, (height, 1), 0)

        def step(j, carry, top=top, tail_cols=tail_cols, tail_rows=tail_rows):
            r = work[pl.ds(j, 1), :]
            whole = work[top:, :]
            col = jnp.sum(jnp.where(tail_cols == j, whole, 0.0), axis=1, keepdims=True)
            piv = jnp.sum(jnp.where(lane == j, r, 0.0), axis=1, keepdims=True)
            inv_piv = 1.0 / piv
            r_live = jnp.where(lane >= j, r, 0.0)
            mult = jnp.where(tail_rows > j, col * inv_piv, 0.0)
            work[top:, :] = whole - mult * r_live
            e_row = elim[pl.ds(j, 1), :]
            elim[top:, :] = elim[top:, :] - mult * e_row
            scale = 1.0 / jnp.sqrt(piv)
            upper[pl.ds(j, 1), :] = r_live * scale
            inv_ref[pl.ds(j, 1), :] = e_row * scale
            return carry

        lax.fori_loop(top, top + phase, step, 0)
    l_ref[...] = jnp.transpose(upper[...])


def block_chol(a):
    n = a.shape[-1]
    return pl.pallas_call(
        block_chol_kernel,
        out_shape=(jax.ShapeDtypeStruct((n, n), jnp.float32), jax.ShapeDtypeStruct((n, n), jnp.float32)),
        in_specs=[pl.BlockSpec(memory_space=pltpu.VMEM)],
        out_specs=(pl.BlockSpec(memory_space=pltpu.VMEM), pl.BlockSpec(memory_space=pltpu.VMEM)),
        scratch_shapes=[pltpu.VMEM((n, n), jnp.float32)] * 3,
    )(a)


def chunks_out_kernel(x_ref, y_ref, send_sem, recv_sem, own_sem, *, count):
    me = lax.axis_index("narrow")
    wide = lax.axis_index("wide")
    barrier = pltpu.get_barrier_semaphore()
    for d in range(1, count):
        peer = lax.rem(me + d, count)
        pl.semaphore_signal(barrier, inc=1, device_id=(wide, peer), device_id_type=MESH)
    pl.semaphore_wait(barrier, count - 1)
    own = pltpu.make_async_copy(x_ref.at[me], y_ref.at[me], own_sem)
    own.start()
    copies = []
    for d in range(1, count):
        peer = lax.rem(me + d, count)
        copy = pltpu.make_async_remote_copy(
            src_ref=x_ref.at[peer],
            dst_ref=y_ref.at[me],
            send_sem=send_sem.at[d - 1],
            recv_sem=recv_sem.at[d - 1],
            device_id=(wide, peer),
            device_id_type=MESH,
        )
        copy.start()
        copies.append(copy)
    own.wait()
    for copy in copies:
        copy.wait()


def chunks_out(x, collective_id):
    count = x.shape[0]
    return pl.pallas_call(
        functools.partial(chunks_out_kernel, count=count),
        out_shape=jax.ShapeDtypeStruct(x.shape, x.dtype),
        in_specs=[pl.BlockSpec(memory_space=pl.ANY)],
        out_specs=pl.BlockSpec(memory_space=pl.ANY),
        scratch_shapes=[
            pltpu.SemaphoreType.DMA((count - 1,)),
            pltpu.SemaphoreType.DMA((count - 1,)),
            pltpu.SemaphoreType.DMA,
        ],
        compiler_params=pltpu.CompilerParams(collective_id=collective_id, has_side_effects=True),
        cost_estimate=pl.CostEstimate(flops=0, bytes_accessed=2 * x.size * 4, transcendentals=0),
    )(x)


def quarters_out_kernel(x_ref, y_ref, send_sem, recv_sem, own_sem, *, count, group, height):
    me = lax.axis_index("narrow")
    wide = lax.axis_index("wide")
    barrier = pltpu.get_barrier_semaphore()
    for d in range(1, count):
        peer = lax.rem(me + d, count)
        pl.semaphore_signal(barrier, inc=1, device_id=(wide, peer), device_id_type=MESH)
    pl.semaphore_wait(barrier, count - 1)
    mine = y_ref.at[pl.ds(me * group, group)]
    own = pltpu.make_async_copy(
        x_ref.at[:, :, pl.ds(pl.multiple_of(me * height, height), height), :], mine, own_sem
    )
    own.start()
    copies = []
    for d in range(1, count):
        peer = lax.rem(me + d, count)
        copy = pltpu.make_async_remote_copy(
            src_ref=x_ref.at[:, :, pl.ds(pl.multiple_of(peer * height, height), height), :],
            dst_ref=mine,
            send_sem=send_sem.at[d - 1],
            recv_sem=recv_sem.at[d - 1],
            device_id=(wide, peer),
            device_id_type=MESH,
        )
        copy.start()
        copies.append(copy)
    own.wait()
    for copy in copies:
        copy.wait()


def quarters_out(x, count, collective_id):
    group, pairs, rows, width = x.shape
    height = rows // count
    return pl.pallas_call(
        functools.partial(quarters_out_kernel, count=count, group=group, height=height),
        out_shape=jax.ShapeDtypeStruct((group * count, pairs, height, width), x.dtype),
        in_specs=[pl.BlockSpec(memory_space=pl.ANY)],
        out_specs=pl.BlockSpec(memory_space=pl.ANY),
        scratch_shapes=[
            pltpu.SemaphoreType.DMA((count - 1,)),
            pltpu.SemaphoreType.DMA((count - 1,)),
            pltpu.SemaphoreType.DMA,
        ],
        compiler_params=pltpu.CompilerParams(collective_id=collective_id, has_side_effects=True),
        cost_estimate=pl.CostEstimate(flops=0, bytes_accessed=2 * x.size * 4, transcendentals=0),
    )(x)


def mm(a, b):
    return jnp.einsum("sik,skj->sij", a, b, precision=lax.Precision.HIGHEST)


def mm_t(a, b):
    return jnp.einsum("sik,sjk->sij", a, b, precision=lax.Precision.HIGHEST)


def blocked_cholesky(matrix):
    batch, size, _ = matrix.shape
    nblk = size // B
    eye = jnp.broadcast_to(jnp.eye(B, dtype=jnp.float32), (batch, B, B))
    trailing = matrix
    diag_l, diag_inv, below = [], [], []
    inverse_rows = []
    for k in range(nblk):
        head = trailing[:, :B, :B]
        pieces = [block_chol(head[b]) for b in range(batch)]
        l_kk = jnp.stack([p[0] for p in pieces])
        i_kk = jnp.stack([p[1] for p in pieces])
        diag_l.append(l_kk)
        diag_inv.append(i_kk)
        if k > 0:
            left = jnp.concatenate([below[j][:, (k - j - 1) * B:(k - j) * B, :] for j in range(k)], axis=2)
            upper = jnp.concatenate(inverse_rows, axis=1)
            rest = -mm(left, upper)
            rest = jnp.concatenate([rest[:, :, :k * B], eye, rest[:, :, (k + 1) * B:]], axis=2)
            inverse_rows.append(mm(i_kk, rest))
        else:
            inverse_rows.append(jnp.concatenate(
                [i_kk, jnp.zeros((batch, B, size - B), jnp.float32)], axis=2))
        if k < nblk - 1:
            panel_k = mm_t(trailing[:, B:, :B], i_kk)
            below.append(panel_k)
            trailing = trailing[:, B:, B:] - mm_t(panel_k, panel_k)
    columns = []
    for k in range(nblk):
        parts = []
        if k > 0:
            parts.append(jnp.zeros((batch, k * B, B), jnp.float32))
        parts.append(diag_l[k])
        if k < nblk - 1:
            parts.append(below[k])
        columns.append(jnp.concatenate(parts, axis=1))
    factor = jnp.concatenate(columns, axis=2)
    inverse = jnp.concatenate(inverse_rows, axis=1)
    return factor, inverse


def local(diag_block, panel, panel_count, pair_owner, pair_slot, ancestor):
    supers_here = diag_block.shape[0]
    col_width = diag_block.shape[2]
    diag_rows = diag_block.shape[1]
    narrow_index = lax.axis_index("narrow")
    narrow_count = lax.axis_size("narrow")
    wide_count = lax.axis_size("wide")
    group = supers_here // narrow_count

    whole_diag = lax.all_to_all(diag_block, "narrow", split_axis=0, concat_axis=2, tiled=True)
    whole_panel = lax.all_to_all(panel, "narrow", split_axis=0, concat_axis=2, tiled=True)

    factor, inverse = blocked_cholesky(whole_diag)
    lower_panel = jnp.einsum(
        "srk,sck->src", whole_panel, inverse, precision=lax.Precision.HIGHEST
    )
    counts = lax.dynamic_slice_in_dim(panel_count, narrow_index * group, group)
    block_index = jnp.arange(P_SIZE * B, dtype=jnp.int32) // B
    live = (block_index[None, :] < counts[:, None]).astype(jnp.float32)
    lower_panel = lower_panel * live[:, :, None]

    first, second = pair_lists(P_SIZE)
    npair = len(first)
    blocks = lower_panel.reshape(group, P_SIZE, B, W)
    gram = jnp.einsum("sxc,syc->sxy", lower_panel, lower_panel, precision=lax.Precision.HIGHEST)
    gram = gram.reshape(group, P_SIZE, B, P_SIZE, B)
    contribution = jnp.moveaxis(gram[:, first, :, second, :], 0, 1)

    quarters = quarters_out(contribution, narrow_count, 3)
    quarter_rows = quarters.shape[2]
    pair_rows = supers_here * npair
    quarters = quarters.reshape(pair_rows, quarter_rows, B)

    capacity = max(2, (pair_rows + wide_count - 1) // wide_count)
    owners = pair_owner[:, 0]
    owner_table = (owners[:, None] == jnp.arange(wide_count, dtype=jnp.int32)[None, :]).astype(
        jnp.int32
    )
    earlier = jnp.cumsum(owner_table, axis=0) - owner_table
    rank_here = jnp.sum(earlier * owner_table, axis=1)
    position = owners * capacity + rank_here
    buffer_rows = wide_count * capacity
    row_slots = T_DEV * narrow_count
    slot_ids = jnp.full((buffer_rows,), -1.0, jnp.float32).at[position].set(
        pair_slot.astype(jnp.float32)
    )
    source_row = jnp.zeros((buffer_rows,), jnp.int32).at[position].set(
        jnp.arange(pair_rows, dtype=jnp.int32)
    )
    filled = jnp.zeros((buffer_rows,), jnp.bool_).at[position].set(True)
    send_buffer = jnp.where(filled[:, None, None], quarters[source_row], 0.0)
    meta = jnp.zeros((wide_count, 8, B), jnp.float32)
    meta = meta.at[:, 0, :capacity].set(slot_ids.reshape(wide_count, capacity))
    send_buffer = jnp.concatenate(
        [send_buffer.reshape(wide_count, capacity * quarter_rows, B), meta], axis=1
    )
    send_buffer, factor, lower_panel = lax.optimization_barrier((send_buffer, factor, lower_panel))
    received = lax.all_to_all(send_buffer, "wide", split_axis=0, concat_axis=0, tiled=True)
    factor_back = columns_out(factor, narrow_count, col_width, 0)
    lower_back = columns_out(lower_panel, narrow_count, col_width, 1)
    received, factor_back, lower_back = lax.optimization_barrier((received, factor_back, lower_back))
    got_slots = received[:, capacity * quarter_rows, :capacity].reshape(buffer_rows)
    got_slots = got_slots.astype(jnp.int32)
    received = received[:, : capacity * quarter_rows, :].reshape(buffer_rows, quarter_rows, B)
    slot_table = (got_slots[:, None] == jnp.arange(row_slots, dtype=jnp.int32)[None, :]).astype(
        jnp.float32
    )
    slot_sums = jnp.sum(slot_table.T[:, :, None, None] * received[None], axis=1)
    slot_sums = slot_sums.reshape(narrow_count, T_DEV, quarter_rows, B)
    arrived = chunks_out(slot_sums, 2)
    summed = jnp.swapaxes(arrived, 0, 1).reshape(T_DEV, B, B)
    return (factor_back, lower_back, ancestor - summed)


def solution(mesh):
    placed = (
        P("wide", None, "narrow"),
        P("wide", None, "narrow"),
        P("wide"),
        P("wide", None),
        P("wide"),
        P(("wide", "narrow"), None, None),
    )
    return jax.shard_map(
        local,
        mesh=mesh,
        in_specs=placed,
        out_specs=(
            P("wide", None, "narrow"),
            P("wide", None, "narrow"),
            P(("wide", "narrow"), None, None),
        ),
        check_vma=False,
    )
```
